32 devices in a mesh: slab: 4 (over y, x), dom: 8 (over z, core).
Axes of the slice: x: 2, y: 2, z: 4, core: 2. Of those that a mesh axis runs over, the one named last changes fastest.
Arguments:
- incoming: float32 [4, 2048, 4, 128], P('slab', 'dom'), may hold values from -8 to 65, as said below
- dest: int32 [4, 2048], P('slab', 'dom'), may hold values from 0 to 2047, as said below
- counts: int32 [8, 16, 64], P('slab', 'dom'), may hold values from 0 to 128, as said below
Outputs:
- density: float32 [8, 16, 64, 128], P('slab', 'dom')
- laplace: float32 [8, 16, 64, 128], P('slab', 'dom')
The draws below stay inside these ranges and needn't reach their ends.
Inputs may be any that keep to these rules, and one draw needn't show every extreme that they name: `incoming`: positions lie inside the cell that dest assigns to their block, and slots beyond a cell's count hold positions too. dest holds each cell id of the slab exactly once; every block goes to a domain at most 2 indices away along dom, counted cyclically; from one domain exactly 64 blocks go to each of four domains and none to the others. `counts`: the lowest quarter of the z cells are full.
All inputs are finite; a program needn't handle non-finite values.
Results may differ from the reference program's by a relative error of at most 0.0003.
Values sent between devices are 32-bit elements; how exact they have to be, the bound alone decides.
No kernel may reach another device: no remote copies, remote signals or barrier semaphores. Data moves between devices by JAX's collectives and lax.ppermute only.
A program may use at most 64 MiB of HBM per device.

```python
import jax
import jax.numpy as jnp
from jax import lax

SLOTS = 128
LX = 2
LY = 2
LZ = 64
CELL_DEV = 256
CAP = 64
CELLS_SLAB = 2048
NX = 8
NY = 16
NZ = 64
N_SLAB = 4
N_DOM = 8


def block_moves(key):
    slab_keys = jax.random.split(jax.random.fold_in(key, 5), N_SLAB)
    offsets = jax.vmap(jax.random.permutation, in_axes=(0, None))(slab_keys, 5)[:, :4] - 2
    sender = jnp.arange(N_DOM, dtype=jnp.int32)
    quarter = jnp.arange(4, dtype=jnp.int32)
    home_dom = (sender[None, :, None] + offsets[:, None, :]) % N_DOM
    cell_ids = home_dom[..., None] * CELL_DEV + quarter[None, None, :, None] * CAP + jnp.arange(CAP, dtype=jnp.int32)[None, None, None, :]
    cell_ids = cell_ids.reshape(N_SLAB * N_DOM, CELL_DEV)
    shuffle_keys = jax.random.split(jax.random.fold_in(key, 6), N_SLAB * N_DOM)
    orders = jax.vmap(jax.random.permutation, in_axes=(0, None))(shuffle_keys, CELL_DEV)
    cell_ids = jnp.take_along_axis(cell_ids, orders, 1)
    return cell_ids.reshape(N_SLAB, N_DOM * CELL_DEV).astype(jnp.int32)


def draw_dest(key, part):
    return block_moves(jax.random.fold_in(key, 71))


def draw_incoming(key, part):
    cell_ids = block_moves(jax.random.fold_in(key, 71))
    float_key = jax.random.fold_in(key, 11)
    owner = cell_ids // CELL_DEV
    within = cell_ids % CELL_DEV
    grid_x = jnp.arange(N_SLAB, dtype=jnp.int32)[:, None] * LX + within // (LY * LZ)
    grid_y = owner * LY + within // LZ % LY
    grid_z = within % LZ
    corner = jnp.stack([grid_x, grid_y, grid_z], 2).astype(jnp.float32)
    jitter = jax.random.uniform(jax.random.fold_in(float_key, 1), (N_SLAB, CELLS_SLAB, 3, SLOTS), jnp.float32)
    position = corner[..., None] + jitter
    field = jnp.clip(jax.random.normal(jax.random.fold_in(float_key, 4), (N_SLAB, CELLS_SLAB, SLOTS), jnp.float32), -6.0, 6.0)
    return jnp.concatenate([position, field[:, :, None, :]], 2).astype(jnp.float32)


def draw_counts(key, part):
    grid_z = jnp.arange(NZ, dtype=jnp.int32)[None, None, :]
    grid_x = jnp.arange(NX, dtype=jnp.int32)[:, None, None]
    fuller = jax.random.randint(jax.random.fold_in(key, 21), (NX, NY, NZ), 64, 129)
    sparse = jax.random.randint(jax.random.fold_in(key, 22), (NX, NY, NZ), 0, 65)
    column = jnp.where(grid_x < NX // 2, fuller, sparse)
    return jnp.where(grid_z < max(NZ // 4, 1), 128, column).astype(jnp.int32)


def setup_inputs(seed: int = 0) -> dict:
    seeds = jax.random.split(jax.random.key(seed), 4)
    incoming = draw_incoming(jax.random.fold_in(seeds[3], 71), 0)
    dest = draw_dest(jax.random.fold_in(seeds[3], 71), 0)
    counts = draw_counts(jax.random.fold_in(seeds[3], 71), 0)
    return dict(incoming=incoming, dest=dest, counts=counts)


radius_eff = 1.0
radius_min = 0.1
ref_density = 268.0825731

def pair_weights(own_cells, own_mask, far_cells, far_mask, diagonal):
    spread = own_cells[:, 0, :, None] - far_cells[:, 0, None, :]
    distance = spread * spread
    for channel in range(1, 3):
        spread = own_cells[:, channel, :, None] - far_cells[:, channel, None, :]
        distance = distance + spread * spread
    radius = jnp.sqrt(jnp.maximum(distance, radius_min * radius_min))
    weight = jnp.maximum(radius_eff / radius - 1.0, 0.0) * own_mask[:, :, None] * far_mask[:, None, :]
    if diagonal:
        weight = weight * (1.0 - jnp.eye(own_mask.shape[1], dtype=weight.dtype))
    return weight

def scatter_blocks(targets, blocks):
    return jnp.zeros_like(blocks).at[targets].set(blocks)

def reference(incoming, dest, counts):
    arranged = jax.vmap(scatter_blocks)(dest, incoming)
    arranged = arranged.reshape(N_SLAB, N_DOM, LX, LY, LZ, 4, SLOTS)
    arranged = arranged.transpose(0, 2, 1, 3, 4, 5, 6).reshape(NX, NY, NZ, 4, SLOTS)
    filled = counts.astype(incoming.dtype)
    padded = jnp.pad(arranged, ((1, 1), (1, 1), (1, 1), (0, 0), (0, 0)))
    padded_count = jnp.pad(filled, 1)
    slot_index = jnp.arange(SLOTS).astype(incoming.dtype)
    anchor = jnp.zeros((), jnp.int32)

    def one_column(column_id):
        row_x = column_id // NY
        row_y = column_id % NY
        own_cells = lax.dynamic_slice(padded, (row_x + 1, row_y + 1, anchor + 1, anchor, anchor), (1, 1, NZ, 4, SLOTS))[0, 0]
        own_count = lax.dynamic_slice(padded_count, (row_x + 1, row_y + 1, anchor + 1), (1, 1, NZ))[0, 0]
        own_mask = (slot_index[None, :] < own_count[:, None]).astype(incoming.dtype)
        total_n = jnp.zeros((NZ, SLOTS), incoming.dtype)
        total_s = jnp.zeros((NZ, SLOTS), incoming.dtype)
        for shift_x in (-1, 0, 1):
            for shift_y in (-1, 0, 1):
                for shift_z in (-1, 0, 1):
                    far_cells = lax.dynamic_slice(padded, (row_x + 1 + shift_x, row_y + 1 + shift_y, anchor + 1 + shift_z, anchor, anchor), (1, 1, NZ, 4, SLOTS))[0, 0]
                    far_count = lax.dynamic_slice(padded_count, (row_x + 1 + shift_x, row_y + 1 + shift_y, anchor + 1 + shift_z), (1, 1, NZ))[0, 0]
                    far_mask = (slot_index[None, :] < far_count[:, None]).astype(incoming.dtype)
                    weight = pair_weights(own_cells, own_mask, far_cells, far_mask, shift_x == 0 and shift_y == 0 and (shift_z == 0))
                    total_n = total_n + weight.sum(2)
                    total_s = total_s + (weight * far_cells[:, 3, None, :]).sum(2)
        return (total_n, total_s)
    sums_n, sums_s = lax.map(one_column, jnp.arange(NX * NY, dtype=jnp.int32))
    sums_n = sums_n.reshape(NX, NY, NZ, SLOTS)
    sums_s = sums_s.reshape(NX, NY, NZ, SLOTS)
    potential = arranged[:, :, :, 3, :]
    density = sums_n / ref_density
    laplace = (sums_s - potential * sums_n) / ref_density
    return (density, laplace)
```

```python
import functools

import jax
import jax.numpy as jnp
from jax import lax
from jax.experimental import pallas as pl
from jax.experimental.pallas import tpu as pltpu
from jax.sharding import PartitionSpec as P

ref_density = 268.0825731
min_square = 0.01
far_away = -1024.0
far_norm = 4096.0
reach = 2
offsets = (-2, -1, 1, 2)

smem = pl.BlockSpec(memory_space=pltpu.SMEM)
vmem = pl.BlockSpec(memory_space=pltpu.VMEM)
params = pltpu.CompilerParams(vmem_limit_bytes=58 * 1024 * 1024)


def pack_kernel(dest, where_am_i, blocks, *refs, cells, capacity, domains):
    outs, home, slots, ids = refs[:4], refs[4], refs[5], refs[6]
    me = where_am_i[1]
    groups = len(offsets)

    def clear(k, _):
        for g in range(groups):
            slots[g, k] = 0
            ids[g, k] = -1
        return 0

    lax.fori_loop(0, capacity, clear, 0)

    def sort_block(b, fill):
        target = dest[b]
        owner = target // cells
        rel = (owner - me + reach + domains) % domains
        stays = rel == reach
        group = jnp.where(rel > reach, rel - 1, rel)
        local = target - owner * cells
        slot = jnp.where(
            stays, fill[4], jnp.where(
                group == 0, fill[0], jnp.where(
                    group == 1, fill[1], jnp.where(group == 2, fill[2], fill[3]))))

        @pl.when(stays)
        def _():
            home[local] = blocks[b]

        @pl.when(jnp.logical_not(stays))
        def _():
            slots[group, slot] = b
            ids[group, slot] = local

        moved = jnp.where(stays, 4, group)
        return tuple(fill[g] + jnp.where(moved == g, 1, 0) for g in range(5))

    lax.fori_loop(0, cells, sort_block, (jnp.int32(0),) * 5)
    lane = lax.broadcasted_iota(jnp.int32, (4, 128), 1) + 128 * lax.broadcasted_iota(
        jnp.int32, (4, 128), 0
    )
    for g in range(groups):

        def copy(k, marks, g=g):
            for u in range(8):
                outs[g][k * 8 + u] = blocks[slots[g, k * 8 + u]]
                marks = jnp.where(lane == k * 8 + u, ids[g, k * 8 + u], marks)
            return marks

        marks = lax.fori_loop(0, capacity // 8, copy, jnp.full((4, 128), -1, jnp.int32))
        outs[g][capacity] = marks.astype(jnp.float32)


def place_kernel(*refs, cells, capacity, levels):
    got, stayed, counts = refs[:4], refs[4], refs[5]
    home, to_dom, to_slab, to_up, to_down = refs[6:11]
    kept, marks, sem = refs[11], refs[12], refs[13]
    copies = [
        pltpu.make_async_copy(got[g].at[capacity], marks.at[g], sem.at[g]) for g in range(4)
    ]
    for copy in copies:
        copy.start()

    def keep(k, _):
        for u in range(8):
            kept[k * 8 + u] = stayed[k * 8 + u]
        return 0

    lax.fori_loop(0, cells // 8, keep, 0)
    for copy in copies:
        copy.wait()
    for g in range(4):

        def put(k, _, g=g):
            for u in range(4):
                slot = k * 4 + u
                cell = marks[g, slot // 128, slot % 128].astype(jnp.int32)

                @pl.when(cell >= 0)
                def _():
                    kept[cell] = got[g][slot]
            return 0

        lax.fori_loop(0, capacity // 4, put, 0)
    lane = lax.broadcasted_iota(jnp.int32, (4, 128), 1)
    row = lax.broadcasted_iota(jnp.int32, (4, 128), 0)
    blank = jnp.where(row == 0, far_away, 0.0)

    def finish(z, _):
        for col in range(4):
            cell = col * levels + z
            block = jnp.where(lane < counts[cell], kept[cell], blank)
            home[cell] = block
            if col == 0:
                to_dom[z] = block
                to_slab[z] = block
                to_up[z] = block
            if col == 1:
                to_slab[levels + z] = block
                to_down[z] = block
            if col == 2:
                to_dom[levels + z] = block
        return 0

    lax.fori_loop(0, levels, finish, 0)


def split3(value):
    high = value.astype(jnp.bfloat16).astype(jnp.float32)
    rest = value - high
    mid = rest.astype(jnp.bfloat16).astype(jnp.float32)
    return high, mid, rest - mid


def load_points(raw, first, corner_x, corner_y, level, valid):
    x = raw[pl.ds(first, 8, 4), :]
    y = raw[pl.ds(first + 1, 8, 4), :]
    z = raw[pl.ds(first + 2, 8, 4), :]
    f = raw[pl.ds(first + 3, 8, 4), :]
    if valid is not None:
        x = jnp.where(valid, x, far_away)
        f = jnp.where(valid, f, 0.0)
    rows = lax.broadcasted_iota(jnp.int32, (8, 128), 0) + level
    return x - corner_x, y - corner_y, z - (rows.astype(jnp.float32) + 0.5), f


def make_lanes(raw, base, col, levels, corner_x, corner_y, valid, flat, side, lanes, values):
    span = levels + 2
    zero = jnp.zeros((8, 128), jnp.float32)
    one = jnp.ones((8, 128), jnp.float32)

    def chunk(k, _):
        level = k * 8
        first = pl.multiple_of((base + level) * 4, 32)
        x, y, z, f = load_points(raw, first, corner_x, corner_y, level, valid)
        values[pl.ds(pl.multiple_of(col * (levels + 16) + 8 + level, 8), 8), :] = f
        x3, y3 = split3(x), split3(y)
        rows = []
        for part in (x3, y3):
            rows += [part[0], part[1], part[0], part[1], part[2], part[0]]
        rows += [one, one, one, zero]
        for r, value in enumerate(rows):
            flat[pl.ds(level * 16 + r, 8, 16), :] = value
        flat_norm = x * x + y * y
        for shift in range(3):
            moved = z + float(shift - 1)
            z3 = split3(moved)
            norm = split3(flat_norm + moved * moved)
            rows = [z3[0], z3[1], z3[0], z3[1], z3[2], z3[0], norm[0], norm[1], norm[2]]
            rows += [zero] * 7
            for r, value in enumerate(rows):
                side[shift, pl.ds(level * 16 + r, 8, 16), :] = value
        return 0

    lax.fori_loop(0, levels // 8, chunk, 0)
    rows16 = lax.broadcasted_iota(jnp.int32, (16, 128), 0)
    empty = jnp.where(rows16 == 6, far_norm, 0.0).astype(jnp.bfloat16)
    for edge in (0, levels + 1):
        lanes[0, col * span + edge] = jnp.zeros((16, 128), jnp.bfloat16)
        for shift in range(3):
            lanes[1 + shift, col * span + edge] = empty
    values[pl.ds(col * (levels + 16), 8), :] = zero
    values[pl.ds(col * (levels + 16) + 8 + levels, 8), :] = zero

    def narrow(k, _):
        for u in range(4):
            z = k * 4 + u
            at = pl.multiple_of(z * 16, 16)
            lanes[0, col * span + 1 + z] = flat[pl.ds(at, 16), :].astype(jnp.bfloat16)
            for shift in range(3):
                lanes[1 + shift, col * span + 1 + z] = side[shift, pl.ds(at, 16), :].astype(
                    jnp.bfloat16
                )
        return 0

    lax.fori_loop(0, levels // 4, narrow, 0)


def make_rows(raw, base, row, levels, corner_x, corner_y, tall, lefts, spread):
    zero = jnp.zeros((8, 128), jnp.float32)
    one = jnp.ones((8, 128), jnp.float32)

    def chunk(k, _):
        level = k * 8
        first = pl.multiple_of((base + level) * 4, 32)
        x, y, z, f = load_points(raw, first, corner_x, corner_y, level, None)
        norm = split3(x * x + y * y + z * z)
        parts = []
        for value in (x, y, z):
            high, mid, low = split3(value)
            high, mid, low = -2.0 * high, -2.0 * mid, -2.0 * low
            parts.append([high, high, mid, mid, high, low])
        rows = parts[0] + parts[1] + [norm[0], norm[1], norm[2], zero]
        rows += parts[2] + [one, one, one] + [zero] * 7 + [f]
        for r, value in enumerate(rows):
            tall[pl.ds(level * 40 + r, 8, 40), :] = value
        return 0

    lax.fori_loop(0, levels // 8, chunk, 0)

    def turn(z, _):
        turned = jnp.transpose(tall[pl.ds(pl.multiple_of(z * 40, 8), 40), :])
        lefts[row * levels + z] = turned[:, :32].astype(jnp.bfloat16)
        spread[row * levels + z] = jnp.broadcast_to(turned[:, 32:33], (128, 128))
        return 0

    lax.fori_loop(0, levels, turn, 0)


def pair_sums(tasks, levels, lefts, spread, lanes, values, col_n, col_s, row_n, row_s, half):
    span = levels + 2
    row_n[...] = jnp.zeros_like(row_n)
    row_s[...] = jnp.zeros_like(row_s)
    col_n[...] = jnp.zeros_like(col_n)
    col_s[...] = jnp.zeros_like(col_s)
    groups = half // 8

    def right(z, tile):
        col, shift, _ = tile
        at = col * span + 1 + z + shift
        return jnp.concatenate([lanes[0, at], lanes[2 + shift, at]], axis=0)

    def level_step(z, _):
        mine = lax.broadcasted_iota(jnp.int32, (half, 128), 1) == z
        for row, tiles in tasks:
            total = None
            fields = []
            for col, shift, _ in tiles:
                f = values[pl.ds(col * (levels + 16) + 8 + z + shift, 1), :]
                fields.append(f)
                total = f if total is None else total + f
            for part in range(128 // half):
                left = lefts[row * levels + z, part * half : (part + 1) * half, :]
                own = [
                    spread[row * levels + z, part * half + g * 8 : part * half + g * 8 + 8, :]
                    for g in range(groups)
                ]
                own_sum = functools.reduce(jnp.add, own)
                sums_n = [jnp.full((8, 128), -float(len(tiles)), jnp.float32)] * groups
                sums_s = [jnp.broadcast_to(-total, (8, 128))] * groups
                for t in range(0, len(tiles), 2):
                    pair = tiles[t : t + 2]
                    rights = [right(z, tile) for tile in pair]
                    square = lax.dot_general(
                        left,
                        jnp.concatenate(rights, axis=1) if len(pair) == 2 else rights[0],
                        (((1,), (0,)), ((), ())),
                        preferred_element_type=jnp.float32,
                    )
                    for p, (col, shift, both) in enumerate(pair):
                        f = fields[t + p]
                        down_n = jnp.full((8, 128), -float(groups), jnp.float32)
                        down_s = -own_sum
                        for g in range(groups):
                            w = lax.rsqrt(
                                jnp.minimum(
                                    jnp.maximum(
                                        square[g * 8 : g * 8 + 8, p * 128 : p * 128 + 128],
                                        min_square,
                                    ),
                                    1.0,
                                )
                            )
                            sums_n[g] = sums_n[g] + w
                            sums_s[g] = sums_s[g] + w * f
                            if both:
                                down_n = down_n + w
                                down_s = down_s + w * own[g]
                        if both:
                            at = pl.ds(pl.multiple_of((col * span + 1 + z + shift) * 8, 8), 8)
                            col_n[at, :] += down_n
                            col_s[at, :] += down_s
                for totals, sums in ((row_n, sums_n), (row_s, sums_s)):
                    for g in range(groups):
                        at = slice(part * half + g * 8, part * half + g * 8 + 8)
                        totals[row, at, :] = jnp.where(
                            mine[:8], jnp.sum(sums[g], axis=1, keepdims=True), totals[row, at, :]
                        )
        return 0

    lax.fori_loop(0, levels, level_step, 0)


def fold_column(ref, col, levels):
    base = (col * (levels + 2) + 1) * 8
    total = None
    for k in range(8):
        part = ref[pl.ds(base + k, levels, 8), :]
        total = part if total is None else total + part
    return total


def own_tasks():
    tasks = []
    for row in range(4):
        tiles = [(row, 0, False), (row, 1, True)]
        for col in range(row + 1, 4):
            tiles += [(col, shift, True) for shift in (-1, 0, 1)]
        tasks.append((row, tiles))
    return tasks


def far_tasks():
    wanted = ((0, (0, 1)), (1, (2, 3, 4)), (2, (0, 1, 3, 4, 5)))
    return [
        (row, [(col, shift, True) for col in cols for shift in (-1, 0, 1)])
        for row, cols in wanted
    ]


def own_kernel(position, raw, out_n, out_s, *scratch, levels, half):
    flat, side, lanes, values, tall, lefts, spread, col_n, col_s, row_n, row_s = scratch
    corner_x = (position[2] + 1).astype(jnp.float32)
    corner_y = (position[3] + 1).astype(jnp.float32)
    for col in range(4):
        make_lanes(
            raw, col * levels, col, levels, corner_x, corner_y, None, flat, side, lanes, values
        )
        make_rows(raw, col * levels, col, levels, corner_x, corner_y, tall, lefts, spread)
    pair_sums(
        own_tasks(), levels, lefts, spread, lanes, values, col_n, col_s, row_n, row_s, half
    )
    for col in range(4):
        f = values[pl.ds(col * (levels + 16) + 8, levels), :]
        itself = lax.rsqrt(jnp.maximum(0.0 * f, min_square)) - 1.0
        out_n[col] = jnp.transpose(row_n[col])[:levels] + fold_column(col_n, col, levels) - itself
        out_s[col] = (
            jnp.transpose(row_s[col])[:levels] + fold_column(col_s, col, levels) - itself * f
        )


def far_kernel(position, raw, dom_raw, slab_raw, up_raw, down_raw, *refs, levels, half):
    out_n, out_s, to_dom, to_slab, to_up, to_down = refs[:6]
    flat, side, lanes, values, tall, lefts, spread, col_n, col_s, row_n, row_s = refs[6:]
    corner_x = (position[2] + 1).astype(jnp.float32)
    corner_y = (position[3] + 1).astype(jnp.float32)
    slab, dom, slabs, doms = position[0], position[1], position[4], position[5]
    next_slab = slab + 1 < slabs
    next_dom = dom + 1 < doms
    previous_dom = dom > 0
    sources = (
        (dom_raw, 0, next_dom),
        (dom_raw, levels, next_dom),
        (down_raw, 0, jnp.logical_and(next_slab, previous_dom)),
        (slab_raw, 0, next_slab),
        (slab_raw, levels, next_slab),
        (up_raw, 0, jnp.logical_and(next_slab, next_dom)),
    )
    for col, (source, base, valid) in enumerate(sources):
        make_lanes(
            source, base, col, levels, corner_x, corner_y, valid, flat, side, lanes, values
        )
    for row in range(3):
        make_rows(raw, (row + 1) * levels, row, levels, corner_x, corner_y, tall, lefts, spread)
    pair_sums(
        far_tasks(), levels, lefts, spread, lanes, values, col_n, col_s, row_n, row_s, half
    )
    for row in range(3):
        out_n[row] = jnp.transpose(row_n[row])[:levels]
        out_s[row] = jnp.transpose(row_s[row])[:levels]
    for channel, ref in enumerate((col_n, col_s)):
        for k in range(2):
            to_dom[channel, k] = fold_column(ref, k, levels)
            to_slab[channel, k] = fold_column(ref, 3 + k, levels)
        to_down[channel] = fold_column(ref, 2, levels)
        to_up[channel] = fold_column(ref, 5, levels)


def finish_kernel(counts, raw, own_n, own_s, far_n, far_s, *refs, levels):
    from_dom, from_slab, from_up, from_down, density, laplace = refs
    lane = lax.broadcasted_iota(jnp.int32, (levels, 128), 1)
    for col in range(4):
        sums = []
        for channel, (near, far) in enumerate(((own_n, far_n), (own_s, far_s))):
            total = near[col]
            if col > 0:
                total = total + far[col - 1]
            if col in (0, 2):
                total = total + from_dom[channel, col // 2]
            if col in (0, 1):
                total = total + from_slab[channel, col]
            if col == 0:
                total = total + from_up[channel]
            if col == 1:
                total = total + from_down[channel]
            sums.append(total)
        filled = lane < counts[col]
        n = jnp.where(filled, sums[0], 0.0)
        s = jnp.where(filled, sums[1], 0.0)
        f = raw[pl.ds(col * levels * 4 + 3, levels, 4), :]
        density[col] = n / ref_density
        laplace[col] = (s - f * n) / ref_density


def scratch_for(levels, cols, rows):
    span = levels + 2
    f32, bf16 = jnp.float32, jnp.bfloat16
    return [
        pltpu.VMEM((levels * 16, 128), f32),
        pltpu.VMEM((3, levels * 16, 128), f32),
        pltpu.VMEM((4, cols * span, 16, 128), bf16),
        pltpu.VMEM((cols * (levels + 16), 128), f32),
        pltpu.VMEM((levels * 40, 128), f32),
        pltpu.VMEM((rows * levels, 128, 32), bf16),
        pltpu.VMEM((rows * levels, 128, 128), f32),
        pltpu.VMEM((cols * span * 8, 128), f32),
        pltpu.VMEM((cols * span * 8, 128), f32),
        pltpu.VMEM((rows, 128, 128), f32),
        pltpu.VMEM((rows, 128, 128), f32),
    ]


def local(incoming, dest, counts):
    cells_x, cells_y, levels = counts.shape
    slots = incoming.shape[3]
    cells = cells_x * cells_y * levels
    capacity = cells // 4
    slabs, doms = lax.axis_size("slab"), lax.axis_size("dom")
    slab, dom = lax.axis_index("slab"), lax.axis_index("dom")
    assert (cells_x, cells_y, slots) == (2, 2, 128) and levels % 8 == 0 and levels <= 128
    assert capacity % 8 == 0 and capacity <= 512 and doms >= 5
    f32 = jnp.float32
    shape = jax.ShapeDtypeStruct
    position = jnp.stack(
        [slab, dom, slab * cells_x, dom * cells_y, jnp.int32(slabs), jnp.int32(doms)]
    ).astype(jnp.int32)
    blocks = incoming.reshape(cells, 4, slots)
    flat_counts = counts.reshape(cells)
    block_bytes = 4 * slots * 4
    *packs, stayed = pl.pallas_call(
        functools.partial(pack_kernel, cells=cells, capacity=capacity, domains=doms),
        out_shape=[shape((capacity + 1, 4, slots), f32)] * 4 + [shape((cells, 4, slots), f32)],
        in_specs=[smem, smem, vmem],
        out_specs=[vmem] * 5,
        scratch_shapes=[pltpu.SMEM((4, capacity), jnp.int32), pltpu.SMEM((4, capacity), jnp.int32)],
        compiler_params=params,
        name="pack",
    )(dest.reshape(cells), position, blocks)
    got = [
        lax.ppermute(pack, "dom", [(i, (i + step) % doms) for i in range(doms)])
        for step, pack in zip(offsets, packs)
    ]
    column = (levels, 4, slots)
    home, to_dom, to_slab, to_up, to_down = pl.pallas_call(
        functools.partial(place_kernel, cells=cells, capacity=capacity, levels=levels),
        out_shape=[shape((cells, 4, slots), f32)]
        + [shape((2 * levels, 4, slots), f32)] * 2
        + [shape(column, f32)] * 2,
        in_specs=[vmem] * 5 + [smem],
        out_specs=[vmem] * 5,
        scratch_shapes=[
            pltpu.VMEM((cells, 4, slots), f32),
            pltpu.SMEM((4, 4, slots), f32),
            pltpu.SemaphoreType.DMA((4,)),
        ],
        compiler_params=params,
        name="place",
    )(*got, stayed, flat_counts)

    both = ("slab", "dom")

    def route(step_slab, step_dom):
        pairs = []
        for s in range(slabs):
            for d in range(doms):
                if 0 <= s + step_slab < slabs and 0 <= d + step_dom < doms:
                    pairs.append((s * doms + d, (s + step_slab) * doms + d + step_dom))
        return pairs

    def send(value, step_slab, step_dom):
        return lax.ppermute(value, both, route(step_slab, step_dom))

    def rows_of(value):
        return value.reshape(-1, slots)

    slab_raw = send(to_slab, -1, 0)
    dom_raw = send(to_dom, 0, -1)
    up_raw = send(to_up, -1, -1)
    down_raw = send(to_down, -1, 1)
    raw = rows_of(home)
    half = 64
    plane = (4, levels, slots)
    tile_flops = 2 * 128 * 128 * 32
    own_n, own_s = pl.pallas_call(
        functools.partial(own_kernel, levels=levels, half=half),
        out_shape=[shape(plane, f32)] * 2,
        in_specs=[smem, vmem],
        out_specs=[vmem] * 2,
        scratch_shapes=scratch_for(levels, 4, 4),
        compiler_params=params,
        cost_estimate=pl.CostEstimate(
            flops=1000 * levels * tile_flops, bytes_accessed=cells * block_bytes, transcendentals=0
        ),
        name="own",
    )(position, raw)
    far_n, far_s, ret_dom, ret_slab, ret_up, ret_down = pl.pallas_call(
        functools.partial(far_kernel, levels=levels, half=half),
        out_shape=[shape((3, levels, slots), f32)] * 2
        + [shape((2, 2, levels, slots), f32)] * 2
        + [shape((2, levels, slots), f32)] * 2,
        in_specs=[smem] + [vmem] * 5,
        out_specs=[vmem] * 6,
        scratch_shapes=scratch_for(levels, 6, 3),
        compiler_params=params,
        name="far",
    )(position, raw, rows_of(dom_raw), rows_of(slab_raw), rows_of(up_raw), rows_of(down_raw))
    from_slab = send(ret_slab, 1, 0)
    from_dom = send(ret_dom, 0, 1)
    from_up = send(ret_up, 1, 1)
    from_down = send(ret_down, 1, -1)
    wide_counts = jnp.broadcast_to(counts.reshape(4, levels, 1), plane)
    density, laplace = pl.pallas_call(
        functools.partial(finish_kernel, levels=levels),
        out_shape=[shape(plane, f32)] * 2,
        in_specs=[vmem] * 10,
        out_specs=[vmem] * 2,
        compiler_params=params,
        name="finish",
    )(wide_counts, raw, own_n, own_s, far_n, far_s, from_dom, from_slab, from_up, from_down)
    final = (cells_x, cells_y, levels, slots)
    return density.reshape(final), laplace.reshape(final)


def solution(mesh):
    in_specs = (P("slab", "dom", None, None), P("slab", "dom"), P("slab", "dom", None))
    out_specs = (P("slab", "dom", None, None), P("slab", "dom", None, None))
    return jax.shard_map(local, mesh=mesh, in_specs=in_specs, out_specs=out_specs, check_vma=False)
```

```python
import functools

import jax
import jax.numpy as jnp
from jax import lax
from jax.experimental import pallas as pl
from jax.experimental.pallas import tpu as pltpu
from jax.sharding import PartitionSpec as P

ref_density = 268.0825731
min_square = 0.01
far_away = -1024.0
far_norm = 4096.0
reach = 2
offsets = (-2, -1, 1, 2)

smem = pl.BlockSpec(memory_space=pltpu.SMEM)
vmem = pl.BlockSpec(memory_space=pltpu.VMEM)
params = pltpu.CompilerParams(vmem_limit_bytes=58 * 1024 * 1024)


def pack_kernel(dest, blocks, *refs, cells, capacity, domains):
    outs, home, sorted_blocks, spots, places, sem = refs[:4], *refs[4:9]
    me = lax.axis_index("dom")
    rows = cells // 128
    target = dest[...]
    spot = jnp.zeros((rows, 128), jnp.int32)
    local = jnp.zeros((rows, 128), jnp.int32)
    lane = lax.broadcasted_iota(jnp.int32, (128, 128), 1)
    row = lax.broadcasted_iota(jnp.int32, (128, 128), 0)
    before = jnp.where(row < lane, 1.0, 0.0).astype(jnp.bfloat16)
    whole = jnp.ones((128, 128), jnp.bfloat16)
    for g, step in enumerate(offsets + (0,)):
        owner = lax.rem(me + step + domains, domains)
        within = target - owner * cells
        chosen = jnp.logical_and(within >= 0, within < cells)
        local = jnp.where(chosen, within, local)
        if step == 0:
            rank = within
        else:
            ones = jnp.concatenate(
                [jnp.where(chosen, 1.0, 0.0), jnp.zeros((16 - rows, 128), jnp.float32)], 0
            ).astype(jnp.bfloat16)
            inside = jnp.dot(ones, before, preferred_element_type=jnp.float32)[:rows]
            counted = jnp.dot(ones, whole, preferred_element_type=jnp.float32)[:rows]
            earlier = [jnp.zeros((1, 128), jnp.float32)]
            for r in range(rows - 1):
                earlier.append(earlier[-1] + counted[r : r + 1])
            rank = (inside + jnp.concatenate(earlier, 0)).astype(jnp.int32)
        spot = jnp.where(chosen, g * capacity + rank, spot)
    spots[...] = spot
    copy = pltpu.make_async_copy(spots, places, sem)
    copy.start()
    high = jnp.floor((local + 1).astype(jnp.float32) * (1.0 / 128.0))
    low = (local + 1).astype(jnp.float32) - 128.0 * high
    filler = jnp.zeros((7, 128), jnp.float32)
    sent = 4 * capacity
    marks = [jnp.zeros((8, sent), jnp.float32)] * 2
    slot = lax.broadcasted_iota(jnp.int32, (sent, 128), 0)
    for r in range(rows):
        hit = jnp.where(slot == spot[r : r + 1], 1.0, 0.0).astype(jnp.bfloat16)
        for k, value in enumerate((high, low)):
            marks[k] = marks[k] + lax.dot_general(
                jnp.concatenate([value[r : r + 1], filler], 0).astype(jnp.bfloat16),
                hit,
                (((1,), (1,)), ((), ())),
                preferred_element_type=jnp.float32,
            )
    marks = (128.0 * marks[0] + marks[1])[:1]
    copy.wait()

    def move(k, _):
        for u in range(16):
            b = k * 16 + u
            sorted_blocks[places[b // 128, lax.rem(b, 128)]] = blocks[b]
        return 0

    lax.fori_loop(0, cells // 16, move, 0)
    for g in range(4):
        for k in range(0, capacity, 8):
            outs[g][k : k + 8] = sorted_blocks[g * capacity + k : g * capacity + k + 8]
        for r in range(4):
            at = min(r * 128, sent - 128)
            outs[g][capacity, r : r + 1] = marks[:, at : at + 128]
    home[...] = sorted_blocks[4 * capacity :]


def place_kernel(*refs, cells, capacity, levels):
    got, stayed, counts = refs[:4], refs[4], refs[5]
    home, to_dom, to_slab, to_up, to_down = refs[6:11]
    kept, cell_ids, marks, sem = refs[11:]
    for g in range(4):
        sent = got[g][capacity].astype(jnp.int32) - 1
        cell_ids[g] = jnp.where(sent < 0, cells, sent)
    copy = pltpu.make_async_copy(cell_ids, marks, sem)
    copy.start()
    kept[:cells] = stayed[...]
    copy.wait()
    for g in range(4):

        def put(k, _, g=g):
            for u in range(8):
                slot = k * 8 + u
                spot = g * capacity + slot
                kept[marks[g, spot // 128, lax.rem(spot, 128)]] = got[g][slot]
            return 0

        lax.fori_loop(0, capacity // 8, put, 0)
    lane = lax.broadcasted_iota(jnp.int32, (4, 128), 1)
    row = lax.broadcasted_iota(jnp.int32, (4, 128), 0)
    blank = jnp.where(row == 0, far_away, 0.0)

    def finish(k, _):
        for u in range(4):
            z = k * 4 + u
            for col in range(4):
                cell = col * levels + z
                block = jnp.where(lane < counts[col // 2, col % 2, z], kept[cell], blank)
                home[cell] = block
                if col == 0:
                    to_dom[z] = block
                    to_slab[z] = block
                    to_up[z] = block
                if col == 1:
                    to_slab[levels + z] = block
                    to_down[z] = block
                if col == 2:
                    to_dom[levels + z] = block
        return 0

    lax.fori_loop(0, levels // 4, finish, 0)


def split3(value):
    high = value.astype(jnp.bfloat16).astype(jnp.float32)
    rest = value - high
    mid = rest.astype(jnp.bfloat16).astype(jnp.float32)
    return high, mid, rest - mid


def load_points(raw, first, corner_x, corner_y, level, valid):
    x = raw[pl.ds(first, 8, 4), :]
    y = raw[pl.ds(first + 1, 8, 4), :]
    z = raw[pl.ds(first + 2, 8, 4), :]
    f = raw[pl.ds(first + 3, 8, 4), :]
    if valid is not None:
        x = jnp.where(valid, x, far_away)
        f = jnp.where(valid, f, 0.0)
    rows = lax.broadcasted_iota(jnp.int32, (8, 128), 0) + level
    return x - corner_x, y - corner_y, z - (rows.astype(jnp.float32) + 0.5), f


def make_lanes(raw, base, col, levels, corner_x, corner_y, valid, flat, side, lanes, values):
    span = levels + 2
    zero = jnp.zeros((8, 128), jnp.float32)
    one = jnp.ones((8, 128), jnp.float32)

    def chunk(k, _):
        level = k * 8
        first = pl.multiple_of((base + level) * 4, 32)
        x, y, z, f = load_points(raw, first, corner_x, corner_y, level, valid)
        values[pl.ds(pl.multiple_of(col * (levels + 16) + 8 + level, 8), 8), :] = f
        x3, y3 = split3(x), split3(y)
        rows = []
        for part in (x3, y3):
            rows += [part[0], part[1], part[0], part[1], part[2], part[0]]
        rows += [one, one, one, zero]
        for r, value in enumerate(rows):
            flat[pl.ds(level * 16 + r, 8, 16), :] = value
        flat_norm = x * x + y * y
        for shift in range(3):
            moved = z + float(shift - 1)
            z3 = split3(moved)
            norm = split3(flat_norm + moved * moved)
            rows = [z3[0], z3[1], z3[0], z3[1], z3[2], z3[0], norm[0], norm[1], norm[2]]
            rows += [zero] * 7
            for r, value in enumerate(rows):
                side[shift, pl.ds(level * 16 + r, 8, 16), :] = value
        return 0

    lax.fori_loop(0, levels // 8, chunk, 0)
    rows16 = lax.broadcasted_iota(jnp.int32, (16, 128), 0)
    empty = jnp.where(rows16 == 6, far_norm, 0.0).astype(jnp.bfloat16)
    for edge in (0, levels + 1):
        lanes[0, col * span + edge] = jnp.zeros((16, 128), jnp.bfloat16)
        for shift in range(3):
            lanes[1 + shift, col * span + edge] = empty
    values[pl.ds(col * (levels + 16), 8), :] = zero
    values[pl.ds(col * (levels + 16) + 8 + levels, 8), :] = zero

    def narrow(k, _):
        for u in range(4):
            z = k * 4 + u
            at = pl.multiple_of(z * 16, 16)
            lanes[0, col * span + 1 + z] = flat[pl.ds(at, 16), :].astype(jnp.bfloat16)
            for shift in range(3):
                lanes[1 + shift, col * span + 1 + z] = side[shift, pl.ds(at, 16), :].astype(
                    jnp.bfloat16
                )
        return 0

    lax.fori_loop(0, levels // 4, narrow, 0)


def make_rows(raw, base, row, levels, corner_x, corner_y, tall, lefts):
    zero = jnp.zeros((8, 128), jnp.float32)
    one = jnp.ones((8, 128), jnp.float32)

    def chunk(k, _):
        level = k * 8
        first = pl.multiple_of((base + level) * 4, 32)
        x, y, z, f = load_points(raw, first, corner_x, corner_y, level, None)
        norm = split3(x * x + y * y + z * z)
        parts = []
        for value in (x, y, z):
            high, mid, low = split3(value)
            high, mid, low = -2.0 * high, -2.0 * mid, -2.0 * low
            parts.append([high, high, mid, mid, high, low])
        rows = parts[0] + parts[1] + [norm[0], norm[1], norm[2], zero]
        rows += parts[2] + [one, one, one] + list(split3(f)) + [zero] * 4
        for r, value in enumerate(rows):
            tall[pl.ds(level * 32 + r, 8, 32), :] = value
        return 0

    lax.fori_loop(0, levels // 8, chunk, 0)

    def narrow(k, _):
        for u in range(4):
            z = k * 4 + u
            lefts[row * levels + z] = tall[pl.ds(pl.multiple_of(z * 32, 32), 32), :].astype(
                jnp.bfloat16
            )
        return 0

    lax.fori_loop(0, levels // 4, narrow, 0)


def pair_sums(
    tasks, levels, lefts, lanes, values, col_n, col_s, row_n, row_s, half, unroll
):
    span = levels + 2
    row_n[...] = jnp.zeros_like(row_n)
    row_s[...] = jnp.zeros_like(row_s)
    col_n[...] = jnp.zeros_like(col_n)
    col_s[...] = jnp.zeros_like(col_s)
    groups = half // 8
    spots = lax.broadcasted_iota(jnp.int32, (32, 128), 0)
    picks = jnp.logical_and(spots >= 25, spots < 28)
    field_rows = jnp.where(picks, 1.0, 0.0).astype(jnp.bfloat16)

    def right(z, tile):
        if tile is None:
            return field_rows
        col, shift, _ = tile
        at = col * span + 1 + z + shift
        return jnp.concatenate([lanes[0, at], lanes[2 + shift, at]], axis=0)

    def weights(square):
        return lax.rsqrt(jnp.minimum(jnp.maximum(square, min_square), 1.0))

    def level_step(z):
        mine = lax.broadcasted_iota(jnp.int32, (8, 128), 1) == z
        for row, tiles in tasks:
            total = None
            fields = {}
            for tile in tiles:
                col, shift, _ = tile
                f = values[pl.ds(col * (levels + 16) + 8 + z + shift, 1), :]
                fields[tile] = f
                total = f if total is None else total + f
            queue = [None] + tiles
            whole = jnp.transpose(lefts[row * levels + z])
            for part in range(128 // half):
                left = whole[part * half : (part + 1) * half]
                sums_n = [jnp.full((8, 128), -float(len(tiles)), jnp.float32)] * groups
                sums_s = [jnp.broadcast_to(-total, (8, 128))] * groups
                own = own_sum = None
                for t in range(0, len(queue), 2):
                    pair = queue[t : t + 2]
                    rights = [right(z, tile) for tile in pair]
                    square = lax.dot_general(
                        left,
                        jnp.concatenate(rights, axis=1) if len(pair) == 2 else rights[0],
                        (((1,), (0,)), ((), ())),
                        preferred_element_type=jnp.float32,
                    )
                    for p, tile in enumerate(pair):
                        pieces = [
                            square[g * 8 : g * 8 + 8, p * 128 : p * 128 + 128]
                            for g in range(groups)
                        ]
                        if tile is None:
                            own = pieces
                            own_sum = functools.reduce(jnp.add, own)
                            continue
                        col, shift, both = tile
                        f = fields[tile]
                        down_n = jnp.full((8, 128), -float(groups), jnp.float32)
                        down_s = -own_sum
                        for g in range(groups):
                            w = weights(pieces[g])
                            sums_n[g] = sums_n[g] + w
                            sums_s[g] = sums_s[g] + w * f
                            if both:
                                down_n = down_n + w
                                down_s = down_s + w * own[g]
                        if both:
                            at = pl.ds(pl.multiple_of((col * span + 1 + z + shift) * 8, 8), 8)
                            col_n[at, :] += down_n
                            col_s[at, :] += down_s
                for totals, sums in ((row_n, sums_n), (row_s, sums_s)):
                    for g in range(groups):
                        at = slice(part * half + g * 8, part * half + g * 8 + 8)
                        totals[row, at, :] = jnp.where(
                            mine, jnp.sum(sums[g], axis=1, keepdims=True), totals[row, at, :]
                        )

    def some_levels(k, _):
        for u in range(unroll):
            level_step(k * unroll + u)
        return 0

    lax.fori_loop(0, levels // unroll, some_levels, 0)


def fold_column(ref, col, levels):
    base = (col * (levels + 2) + 1) * 8
    total = None
    for k in range(8):
        part = ref[pl.ds(base + k, levels, 8), :]
        total = part if total is None else total + part
    return total


def own_tasks(rows):
    tasks = []
    for row in rows:
        tiles = [(row, 0, False), (row, 1, True)]
        for col in range(row + 1, 4):
            tiles += [(col, shift, True) for shift in (-1, 0, 1)]
        tasks.append((row, tiles))
    return tasks


def far_tasks():
    wanted = ((0, (0, 1)), (1, (2, 3, 4)), (2, (0, 1, 3, 4, 5)))
    return [
        (row, [(col, shift, True) for col in cols for shift in (-1, 0, 1)])
        for row, cols in wanted
    ]


def corners():
    corner_x = (lax.axis_index("slab") * 2 + 1).astype(jnp.float32)
    corner_y = (lax.axis_index("dom") * 2 + 1).astype(jnp.float32)
    return corner_x, corner_y


def own_kernel(raw, *refs, levels, half, unroll, first, last):
    count = 4 - first
    starts, refs = (refs[:2], refs[2:]) if first else (None, refs)
    (out_n, out_s), scratch = refs[:2], refs[2:]
    flat, side, lanes, values, tall, lefts, col_n, col_s, row_n, row_s = scratch
    corner_x, corner_y = corners()
    for col in range(count):
        base = (col + first) * levels
        make_lanes(raw, base, col, levels, corner_x, corner_y, None, flat, side, lanes, values)
    for row in range(last - first):
        make_rows(raw, (row + first) * levels, row, levels, corner_x, corner_y, tall, lefts)
    tasks = [
        (row - first, [(col - first, shift, both) for col, shift, both in tiles])
        for row, tiles in own_tasks(range(first, last))
    ]
    pair_sums(tasks, levels, lefts, lanes, values, col_n, col_s, row_n, row_s, half, unroll)
    for col in range(4):
        if col < first:
            out_n[col] = starts[0][col]
            out_s[col] = starts[1][col]
            continue
        n = fold_column(col_n, col - first, levels)
        s = fold_column(col_s, col - first, levels)
        if col < last:
            f = values[pl.ds((col - first) * (levels + 16) + 8, levels), :]
            itself = lax.rsqrt(jnp.maximum(0.0 * f, min_square)) - 1.0
            n = n + jnp.transpose(row_n[col - first])[:levels] - itself
            s = s + jnp.transpose(row_s[col - first])[:levels] - itself * f
        if first:
            n = n + starts[0][col]
            s = s + starts[1][col]
        out_n[col] = n
        out_s[col] = s


def far_kernel(raw, dom_raw, slab_raw, up_raw, down_raw, *refs, levels, half, unroll, slabs, doms):
    start_n, start_s, out_n, out_s, to_dom, to_slab, to_up, to_down = refs[:8]
    flat, side, lanes, values, tall, lefts, col_n, col_s, row_n, row_s = refs[8:]
    corner_x, corner_y = corners()
    slab, dom = lax.axis_index("slab"), lax.axis_index("dom")
    next_slab = slab + 1 < slabs
    next_dom = dom + 1 < doms
    previous_dom = dom > 0
    sources = (
        (dom_raw, 0, next_dom),
        (dom_raw, levels, next_dom),
        (down_raw, 0, jnp.logical_and(next_slab, previous_dom)),
        (slab_raw, 0, next_slab),
        (slab_raw, levels, next_slab),
        (up_raw, 0, jnp.logical_and(next_slab, next_dom)),
    )
    for col, (source, base, valid) in enumerate(sources):
        make_lanes(
            source, base, col, levels, corner_x, corner_y, valid, flat, side, lanes, values
        )
    for row in range(3):
        make_rows(raw, (row + 1) * levels, row, levels, corner_x, corner_y, tall, lefts)
    pair_sums(
        far_tasks(), levels, lefts, lanes, values, col_n, col_s, row_n, row_s, half, unroll
    )
    out_n[0] = start_n[0]
    out_s[0] = start_s[0]
    for row in range(3):
        out_n[row + 1] = start_n[row + 1] + jnp.transpose(row_n[row])[:levels]
        out_s[row + 1] = start_s[row + 1] + jnp.transpose(row_s[row])[:levels]
    for channel, ref in enumerate((col_n, col_s)):
        for k in range(2):
            to_dom[channel, k] = fold_column(ref, k, levels)
            to_slab[channel, k] = fold_column(ref, 3 + k, levels)
        to_down[channel] = fold_column(ref, 2, levels)
        to_up[channel] = fold_column(ref, 5, levels)


def finish_kernel(raw, own_n, own_s, *refs, levels):
    from_dom, from_slab, from_up, from_down, density, laplace = refs
    for col in range(4):
        sums = []
        for channel, near in enumerate((own_n, own_s)):
            total = near[col]
            if col in (0, 2):
                total = total + from_dom[channel, col // 2]
            if col in (0, 1):
                total = total + from_slab[channel, col]
            if col == 0:
                total = total + from_up[channel]
            if col == 1:
                total = total + from_down[channel]
            sums.append(total)
        filled = raw[pl.ds(col * levels * 4, levels, 4), :] > 0.5 * far_away
        n = jnp.where(filled, sums[0], 0.0)
        s = jnp.where(filled, sums[1], 0.0)
        f = raw[pl.ds(col * levels * 4 + 3, levels, 4), :]
        density[col] = n / ref_density
        laplace[col] = (s - f * n) / ref_density


def scratch_for(levels, cols, rows):
    span = levels + 2
    f32, bf16 = jnp.float32, jnp.bfloat16
    return [
        pltpu.VMEM((levels * 16, 128), f32),
        pltpu.VMEM((3, levels * 16, 128), f32),
        pltpu.VMEM((4, cols * span, 16, 128), bf16),
        pltpu.VMEM((cols * (levels + 16), 128), f32),
        pltpu.VMEM((levels * 32, 128), f32),
        pltpu.VMEM((rows * levels, 32, 128), bf16),
        pltpu.VMEM((cols * span * 8, 128), f32),
        pltpu.VMEM((cols * span * 8, 128), f32),
        pltpu.VMEM((rows, 128, 128), f32),
        pltpu.VMEM((rows, 128, 128), f32),
    ]


def local(incoming, dest, counts):
    cells_x, cells_y, levels = counts.shape
    slots = incoming.shape[3]
    cells = cells_x * cells_y * levels
    capacity = cells // 4
    slabs, doms = lax.axis_size("slab"), lax.axis_size("dom")
    assert (cells_x, cells_y, slots) == (2, 2, 128) and levels % 8 == 0 and levels <= 128
    assert cells % 128 == 0 and cells <= 16 * 128 and doms >= 5
    assert capacity % 8 == 0 and 128 <= 4 * capacity <= 512
    f32, i32 = jnp.float32, jnp.int32
    shape = jax.ShapeDtypeStruct
    blocks = incoming.reshape(cells, 4, slots)
    *packs, stayed = pl.pallas_call(
        functools.partial(pack_kernel, cells=cells, capacity=capacity, domains=doms),
        out_shape=[shape((capacity + 1, 4, slots), f32)] * 4 + [shape((cells, 4, slots), f32)],
        in_specs=[vmem, vmem],
        out_specs=[vmem] * 5,
        scratch_shapes=[
            pltpu.VMEM((4 * capacity + cells, 4, slots), f32),
            pltpu.VMEM((cells // 128, 128), i32),
            pltpu.SMEM((cells // 128, 128), i32),
            pltpu.SemaphoreType.DMA,
        ],
        compiler_params=params,
        name="pack",
    )(dest.reshape(cells // 128, 128), blocks)
    got = [
        lax.ppermute(pack, "dom", [(i, (i + step) % doms) for i in range(doms)])
        for step, pack in zip(offsets, packs)
    ]
    column = (levels, 4, slots)
    home, to_dom, to_slab, to_up, to_down = pl.pallas_call(
        functools.partial(place_kernel, cells=cells, capacity=capacity, levels=levels),
        out_shape=[shape((cells, 4, slots), f32)]
        + [shape((2 * levels, 4, slots), f32)] * 2
        + [shape(column, f32)] * 2,
        in_specs=[vmem] * 5 + [smem],
        out_specs=[vmem] * 5,
        scratch_shapes=[
            pltpu.VMEM((cells + 1, 4, slots), f32),
            pltpu.VMEM((4, 4, 128), i32),
            pltpu.SMEM((4, 4, 128), i32),
            pltpu.SemaphoreType.DMA,
        ],
        compiler_params=params,
        name="place",
    )(*got, stayed, counts)

    both = ("slab", "dom")

    def route(step_slab, step_dom):
        pairs = []
        for s in range(slabs):
            for d in range(doms):
                if 0 <= s + step_slab < slabs and 0 <= d + step_dom < doms:
                    pairs.append((s * doms + d, (s + step_slab) * doms + d + step_dom))
        return pairs

    def send(value, step_slab, step_dom):
        return lax.ppermute(value, both, route(step_slab, step_dom))

    def rows_of(value):
        return value.reshape(-1, slots)

    slab_raw = send(to_slab, -1, 0)
    dom_raw = send(to_dom, 0, -1)
    up_raw = send(to_up, -1, -1)
    down_raw = send(to_down, -1, 1)
    raw = rows_of(home)
    half = 128
    plane = (4, levels, slots)

    def cost(tiles):
        return pl.CostEstimate(
            flops=levels * tiles * 128 * 128 * 600,
            bytes_accessed=cells * 4 * slots * 4,
            transcendentals=0,
        )

    def own_pairs(first, last, unroll, *start):
        return pl.pallas_call(
            functools.partial(
                own_kernel, levels=levels, half=half, unroll=unroll, first=first, last=last
            ),
            out_shape=[shape(plane, f32)] * 2,
            in_specs=[vmem] * (1 + len(start)),
            out_specs=[vmem] * 2,
            scratch_shapes=scratch_for(levels, 4 - first, last - first),
            compiler_params=params,
            cost_estimate=cost(26),
            name="own",
        )(raw, *start)

    early_n, early_s = own_pairs(0, 1, 4)
    far_n, far_s, ret_dom, ret_slab, ret_up, ret_down = pl.pallas_call(
        functools.partial(
            far_kernel, levels=levels, half=half, unroll=4, slabs=slabs, doms=doms
        ),
        out_shape=[shape(plane, f32)] * 2
        + [shape((2, 2, levels, slots), f32)] * 2
        + [shape((2, levels, slots), f32)] * 2,
        in_specs=[vmem] * 7,
        out_specs=[vmem] * 6,
        scratch_shapes=scratch_for(levels, 6, 3),
        compiler_params=params,
        cost_estimate=cost(30),
        name="far",
    )(
        raw,
        rows_of(dom_raw),
        rows_of(slab_raw),
        rows_of(up_raw),
        rows_of(down_raw),
        early_n,
        early_s,
    )
    from_slab = send(ret_slab, 1, 0)
    from_dom = send(ret_dom, 0, 1)
    from_up = send(ret_up, 1, 1)
    from_down = send(ret_down, 1, -1)
    own_n, own_s = own_pairs(1, 4, 4, far_n, far_s)
    density, laplace = pl.pallas_call(
        functools.partial(finish_kernel, levels=levels),
        out_shape=[shape(plane, f32)] * 2,
        in_specs=[vmem] * 7,
        out_specs=[vmem] * 2,
        compiler_params=params,
        name="finish",
    )(raw, own_n, own_s, from_dom, from_slab, from_up, from_down)
    final = (cells_x, cells_y, levels, slots)
    return density.reshape(final), laplace.reshape(final)


def solution(mesh):
    in_specs = (P("slab", "dom", None, None), P("slab", "dom"), P("slab", "dom", None))
    out_specs = (P("slab", "dom", None, None), P("slab", "dom", None, None))
    return jax.shard_map(local, mesh=mesh, in_specs=in_specs, out_specs=out_specs, check_vma=False)
```

```python
import functools

import jax
import jax.numpy as jnp
from jax import lax
from jax.experimental import pallas as pl
from jax.experimental.pallas import tpu as pltpu
from jax.sharding import PartitionSpec as P

ref_density = 268.0825731
min_square = 0.01
far_away = -1024.0
far_norm = 4096.0
reach = 2
offsets = (-2, -1, 1, 2)

smem = pl.BlockSpec(memory_space=pltpu.SMEM)
vmem = pl.BlockSpec(memory_space=pltpu.VMEM)
params = pltpu.CompilerParams(vmem_limit_bytes=58 * 1024 * 1024)


def pack_kernel(dest, blocks, *refs, cells, capacity, domains):
    outs, home, sorted_blocks, spots, places, sem = refs[:4], *refs[4:9]
    me = lax.axis_index("dom")
    rows = cells // 128
    target = dest[...]
    spot = jnp.zeros((rows, 128), jnp.int32)
    local = jnp.zeros((rows, 128), jnp.int32)
    lane = lax.broadcasted_iota(jnp.int32, (128, 128), 1)
    row = lax.broadcasted_iota(jnp.int32, (128, 128), 0)
    before = jnp.where(row < lane, 1.0, 0.0).astype(jnp.bfloat16)
    whole = jnp.ones((128, 128), jnp.bfloat16)
    for g, step in enumerate(offsets + (0,)):
        owner = lax.rem(me + step + domains, domains)
        within = target - owner * cells
        chosen = jnp.logical_and(within >= 0, within < cells)
        local = jnp.where(chosen, within, local)
        if step == 0:
            rank = within
        else:
            ones = jnp.concatenate(
                [jnp.where(chosen, 1.0, 0.0), jnp.zeros((16 - rows, 128), jnp.float32)], 0
            ).astype(jnp.bfloat16)
            inside = jnp.dot(ones, before, preferred_element_type=jnp.float32)[:rows]
            counted = jnp.dot(ones, whole, preferred_element_type=jnp.float32)[:rows]
            earlier = [jnp.zeros((1, 128), jnp.float32)]
            for r in range(rows - 1):
                earlier.append(earlier[-1] + counted[r : r + 1])
            rank = (inside + jnp.concatenate(earlier, 0)).astype(jnp.int32)
        spot = jnp.where(chosen, g * capacity + rank, spot)
    spots[...] = spot
    copy = pltpu.make_async_copy(spots, places, sem)
    copy.start()
    high = jnp.floor((local + 1).astype(jnp.float32) * (1.0 / 128.0))
    low = (local + 1).astype(jnp.float32) - 128.0 * high
    filler = jnp.zeros((7, 128), jnp.float32)
    sent = 4 * capacity
    marks = [jnp.zeros((8, sent), jnp.float32)] * 2
    slot = lax.broadcasted_iota(jnp.int32, (sent, 128), 0)
    for r in range(rows):
        hit = jnp.where(slot == spot[r : r + 1], 1.0, 0.0).astype(jnp.bfloat16)
        for k, value in enumerate((high, low)):
            marks[k] = marks[k] + lax.dot_general(
                jnp.concatenate([value[r : r + 1], filler], 0).astype(jnp.bfloat16),
                hit,
                (((1,), (1,)), ((), ())),
                preferred_element_type=jnp.float32,
            )
    marks = (128.0 * marks[0] + marks[1])[:1]
    copy.wait()

    def move(k, _):
        for u in range(16):
            b = k * 16 + u
            sorted_blocks[places[b // 128, lax.rem(b, 128)]] = blocks[b]
        return 0

    lax.fori_loop(0, cells // 16, move, 0)
    for g in range(4):
        for k in range(0, capacity, 8):
            outs[g][k : k + 8] = sorted_blocks[g * capacity + k : g * capacity + k + 8]
        for r in range(4):
            at = min(r * 128, sent - 128)
            outs[g][capacity, r : r + 1] = marks[:, at : at + 128]
    home[...] = sorted_blocks[4 * capacity :]


def place_kernel(*refs, cells, capacity, levels):
    got, stayed, counts = refs[:4], refs[4], refs[5]
    home, to_dom, to_slab, to_edge = refs[6:10]
    kept, cell_ids, marks, sem = refs[10:]
    for g in range(4):
        sent = got[g][capacity].astype(jnp.int32) - 1
        cell_ids[g] = jnp.where(sent < 0, cells, sent)
    copy = pltpu.make_async_copy(cell_ids, marks, sem)
    copy.start()
    kept[:cells] = stayed[...]
    copy.wait()
    for g in range(4):

        def put(k, _, g=g):
            for u in range(8):
                slot = k * 8 + u
                spot = g * capacity + slot
                kept[marks[g, spot // 128, lax.rem(spot, 128)]] = got[g][slot]
            return 0

        lax.fori_loop(0, capacity // 8, put, 0)
    lane = lax.broadcasted_iota(jnp.int32, (4, 128), 1)
    row = lax.broadcasted_iota(jnp.int32, (4, 128), 0)
    blank = jnp.where(row == 0, far_away, 0.0)

    def finish(k, _):
        for u in range(4):
            z = k * 4 + u
            for col in range(4):
                cell = col * levels + z
                block = jnp.where(lane < counts[col // 2, col % 2, z], kept[cell], blank)
                home[cell] = block
                if col == 0:
                    to_dom[z] = block
                    to_slab[z] = block
                    to_edge[z] = block
                if col == 1:
                    to_slab[levels + z] = block
                if col == 2:
                    to_dom[levels + z] = block
        return 0

    lax.fori_loop(0, levels // 4, finish, 0)


def split3(value):
    high = value.astype(jnp.bfloat16).astype(jnp.float32)
    rest = value - high
    mid = rest.astype(jnp.bfloat16).astype(jnp.float32)
    return high, mid, rest - mid


def load_points(raw, first, corner_x, corner_y, level, valid):
    x = raw[pl.ds(first, 8, 4), :]
    y = raw[pl.ds(first + 1, 8, 4), :]
    z = raw[pl.ds(first + 2, 8, 4), :]
    f = raw[pl.ds(first + 3, 8, 4), :]
    if valid is not None:
        x = jnp.where(valid, x, far_away)
        f = jnp.where(valid, f, 0.0)
    rows = lax.broadcasted_iota(jnp.int32, (8, 128), 0) + level
    return x - corner_x, y - corner_y, z - (rows.astype(jnp.float32) + 0.5), f


def make_lanes(raw, base, col, levels, corner_x, corner_y, valid, parts, lanes, values):
    span = levels + 2
    rows = lax.broadcasted_iota(jnp.int32, (8, 128), 0)
    zero = jnp.zeros((8, 128), jnp.float32)

    def chunk(k, _):
        level = pl.multiple_of(k * 8, 8)
        first = pl.multiple_of((base + level) * 4, 32)
        x, y, z, f = load_points(raw, first, corner_x, corner_y, level, valid)
        values[pl.ds(pl.multiple_of(col * (levels + 16) + 8 + level, 8), 8), :] = f
        found = [*split3(x), *split3(y)]
        flat_norm = x * x + y * y
        for shift in range(3):
            moved = z + float(shift - 1)
            found += [*split3(moved), *split3(flat_norm + moved * moved)]
        for p, value in enumerate(found):
            parts[p, pl.ds(level, 8), :] = value
        return 0

    lax.fori_loop(0, levels // 8, chunk, 0)
    rows16 = lax.broadcasted_iota(jnp.int32, (16, 128), 0)
    empty = jnp.where(rows16 == 6, far_norm, 0.0).astype(jnp.bfloat16)
    for edge in (0, levels + 1):
        lanes[0, col * span + edge] = jnp.zeros((16, 128), jnp.bfloat16)
        for shift in range(3):
            lanes[1 + shift, col * span + edge] = empty
    values[pl.ds(col * (levels + 16), 8), :] = zero
    values[pl.ds(col * (levels + 16) + 8 + levels, 8), :] = zero

    def is_in(*which):
        return functools.reduce(jnp.logical_or, [rows == r for r in which])

    mids, low, third, head = is_in(1, 3, 7), is_in(4), is_in(2), is_in(0)
    tail = rows >= 6
    units = jnp.where(rows < 7, 1.0, 0.0)

    def narrow(k, _):
        for u in range(4):
            z = k * 4 + u

            def part(p, z=z):
                return jnp.broadcast_to(parts[p, pl.ds(z, 1), :], (8, 128))

            def six(first, then):
                high = jnp.where(tail, part(then), part(first))
                mid = jnp.where(tail, part(then + 1), part(first + 1))
                return jnp.where(mids, mid, jnp.where(low, part(first + 2), high))

            upper = six(0, 3)
            lower = jnp.where(is_in(1), part(4), jnp.where(third, part(5), part(3)))
            lower = jnp.where(rows >= 4, units, lower)
            at = col * span + 1 + z
            lanes[0, at] = jnp.concatenate([upper, lower], 0).astype(jnp.bfloat16)
            for shift in range(3):
                p = 6 + shift * 6
                upper = six(p, p + 3)
                lower = jnp.where(head, part(p + 5), zero)
                lanes[1 + shift, at] = jnp.concatenate([upper, lower], 0).astype(jnp.bfloat16)
        return 0

    lax.fori_loop(0, levels // 4, narrow, 0)


def make_rows(raw, base, row, levels, corner_x, corner_y, valid, parts, lefts):
    rows = lax.broadcasted_iota(jnp.int32, (8, 128), 0)

    def chunk(k, _):
        level = pl.multiple_of(k * 8, 8)
        first = pl.multiple_of((base + level) * 4, 32)
        x, y, z, f = load_points(raw, first, corner_x, corner_y, level, valid)
        found = []
        for value in (x, y, z):
            found += [-2.0 * part for part in split3(value)]
        found += [*split3(x * x + y * y + z * z), *split3(f)]
        for p, value in enumerate(found):
            parts[p, pl.ds(level, 8), :] = value
        return 0

    lax.fori_loop(0, levels // 8, chunk, 0)

    def pick(choices):
        value = choices[-1][1]
        for which, other in choices[:-1]:
            hit = functools.reduce(jnp.logical_or, [rows == r for r in which])
            value = jnp.where(hit, other, value)
        return value

    def narrow(k, _):
        for u in range(4):
            z = k * 4 + u

            def part(p, z=z):
                return jnp.broadcast_to(parts[p, pl.ds(z, 1), :], (8, 128))

            tile = [
                pick([((2, 3), part(1)), ((5,), part(2)), ((6, 7), part(3)), ((), part(0))]),
                pick(
                    [
                        ((0, 1), part(4)),
                        ((2,), part(3)),
                        ((3,), part(5)),
                        ((4,), part(9)),
                        ((5,), part(10)),
                        ((6,), part(11)),
                        ((), jnp.zeros((8, 128), jnp.float32)),
                    ]
                ),
                pick(
                    [
                        ((2, 3), part(7)),
                        ((5,), part(8)),
                        ((6, 7), jnp.ones((8, 128), jnp.float32)),
                        ((), part(6)),
                    ]
                ),
                pick(
                    [
                        ((1,), part(12)),
                        ((2,), part(13)),
                        ((3,), part(14)),
                        ((), jnp.where(rows == 0, 1.0, 0.0)),
                    ]
                ),
            ]
            lefts[row * levels + z] = jnp.concatenate(tile, 0).astype(jnp.bfloat16)
        return 0

    lax.fori_loop(0, levels // 4, narrow, 0)


def pair_sums(
    tasks, levels, lefts, lanes, values, col_n, col_s, row_n, row_s, half, unroll
):
    span = levels + 2
    row_n[...] = jnp.zeros_like(row_n)
    row_s[...] = jnp.zeros_like(row_s)
    col_n[...] = jnp.zeros_like(col_n)
    col_s[...] = jnp.zeros_like(col_s)
    groups = half // 8
    spots = lax.broadcasted_iota(jnp.int32, (32, 128), 0)
    picks = jnp.logical_and(spots >= 25, spots < 28)
    field_rows = jnp.where(picks, 1.0, 0.0).astype(jnp.bfloat16)

    def right(z, tile):
        if tile is None:
            return field_rows
        col, shift, _ = tile
        at = col * span + 1 + z + shift
        return jnp.concatenate([lanes[0, at], lanes[2 + shift, at]], axis=0)

    def weights(square):
        return lax.rsqrt(jnp.minimum(jnp.maximum(square, min_square), 1.0))

    def level_step(z):
        mine = lax.broadcasted_iota(jnp.int32, (8, 128), 1) == z
        for row, tiles in tasks:
            total = None
            fields = {}
            for tile in tiles:
                col, shift, _ = tile
                f = values[pl.ds(col * (levels + 16) + 8 + z + shift, 1), :]
                fields[tile] = f
                total = f if total is None else total + f
            queue = [None] + tiles
            whole = jnp.transpose(lefts[row * levels + z])
            for part in range(128 // half):
                left = whole[part * half : (part + 1) * half]
                sums_n = [jnp.full((8, 128), -float(len(tiles)), jnp.float32)] * groups
                sums_s = [jnp.broadcast_to(-total, (8, 128))] * groups
                own = own_sum = None
                for t in range(0, len(queue), 2):
                    pair = queue[t : t + 2]
                    rights = [right(z, tile) for tile in pair]
                    square = lax.dot_general(
                        left,
                        jnp.concatenate(rights, axis=1) if len(pair) == 2 else rights[0],
                        (((1,), (0,)), ((), ())),
                        preferred_element_type=jnp.float32,
                    )
                    for p, tile in enumerate(pair):
                        pieces = [
                            square[g * 8 : g * 8 + 8, p * 128 : p * 128 + 128]
                            for g in range(groups)
                        ]
                        if tile is None:
                            own = pieces
                            own_sum = functools.reduce(jnp.add, own)
                            continue
                        col, shift, both = tile
                        f = fields[tile]
                        down_n = jnp.full((8, 128), -float(groups), jnp.float32)
                        down_s = -own_sum
                        for g in range(groups):
                            w = weights(pieces[g])
                            sums_n[g] = sums_n[g] + w
                            sums_s[g] = sums_s[g] + w * f
                            if both:
                                down_n = down_n + w
                                down_s = down_s + w * own[g]
                        if both:
                            at = pl.ds(pl.multiple_of((col * span + 1 + z + shift) * 8, 8), 8)
                            col_n[at, :] += down_n
                            col_s[at, :] += down_s
                for totals, sums in ((row_n, sums_n), (row_s, sums_s)):
                    for g in range(groups):
                        at = slice(part * half + g * 8, part * half + g * 8 + 8)
                        totals[row, at, :] = jnp.where(
                            mine, jnp.sum(sums[g], axis=1, keepdims=True), totals[row, at, :]
                        )

    def some_levels(k, _):
        for u in range(unroll):
            level_step(k * unroll + u)
        return 0

    lax.fori_loop(0, levels // unroll, some_levels, 0)


def fold_column(ref, col, levels):
    base = (col * (levels + 2) + 1) * 8
    total = None
    for k in range(8):
        part = ref[pl.ds(base + k, levels, 8), :]
        total = part if total is None else total + part
    return total


def own_tasks(rows):
    tasks = []
    for row in rows:
        tiles = [(row, 0, False), (row, 1, True)]
        for col in range(row + 1, 4):
            tiles += [(col, shift, True) for shift in (-1, 0, 1)]
        tasks.append((row, tiles))
    return tasks


def far_tasks():
    wanted = ((0, (0, 1)), (1, (2, 3)), (2, (0, 1, 2, 3, 4)), (3, (1,)))
    return [
        (row, [(col, shift, True) for col in cols for shift in (-1, 0, 1)])
        for row, cols in wanted
    ]


def corners():
    corner_x = (lax.axis_index("slab") * 2 + 1).astype(jnp.float32)
    corner_y = (lax.axis_index("dom") * 2 + 1).astype(jnp.float32)
    return corner_x, corner_y


def own_kernel(raw, *refs, levels, half, unroll, first, last):
    count = 4 - first
    starts, refs = (refs[:2], refs[2:]) if first else (None, refs)
    (out_n, out_s), scratch = refs[:2], refs[2:]
    parts, lanes, values, lefts, col_n, col_s, row_n, row_s = scratch
    corner_x, corner_y = corners()
    for col in range(count):
        base = (col + first) * levels
        make_lanes(raw, base, col, levels, corner_x, corner_y, None, parts, lanes, values)
    for row in range(last - first):
        make_rows(
            raw, (row + first) * levels, row, levels, corner_x, corner_y, None, parts, lefts
        )
    tasks = [
        (row - first, [(col - first, shift, both) for col, shift, both in tiles])
        for row, tiles in own_tasks(range(first, last))
    ]
    pair_sums(tasks, levels, lefts, lanes, values, col_n, col_s, row_n, row_s, half, unroll)
    for col in range(4):
        if col < first:
            out_n[col] = starts[0][col]
            out_s[col] = starts[1][col]
            continue
        n = fold_column(col_n, col - first, levels)
        s = fold_column(col_s, col - first, levels)
        if col < last:
            f = values[pl.ds((col - first) * (levels + 16) + 8, levels), :]
            itself = lax.rsqrt(jnp.maximum(0.0 * f, min_square)) - 1.0
            n = n + jnp.transpose(row_n[col - first])[:levels] - itself
            s = s + jnp.transpose(row_s[col - first])[:levels] - itself * f
        if first:
            n = n + starts[0][col]
            s = s + starts[1][col]
        out_n[col] = n
        out_s[col] = s


def far_kernel(raw, dom_raw, slab_raw, edge_raw, *refs, levels, half, unroll, slabs, doms):
    start_n, start_s, out_n, out_s, to_dom, to_slab, to_edge = refs[:7]
    parts, lanes, values, lefts, col_n, col_s, row_n, row_s = refs[7:]
    corner_x, corner_y = corners()
    next_slab = lax.axis_index("slab") + 1 < slabs
    next_dom = lax.axis_index("dom") + 1 < doms
    sources = (
        (dom_raw, 0, next_dom),
        (dom_raw, levels, next_dom),
        (slab_raw, 0, next_slab),
        (slab_raw, levels, next_slab),
        (edge_raw, 0, jnp.logical_and(next_slab, next_dom)),
    )
    for col, (source, base, valid) in enumerate(sources):
        make_lanes(source, base, col, levels, corner_x, corner_y, valid, parts, lanes, values)
    for row in range(3):
        make_rows(raw, (row + 1) * levels, row, levels, corner_x, corner_y, None, parts, lefts)
    make_rows(slab_raw, levels, 3, levels, corner_x, corner_y, next_slab, parts, lefts)
    pair_sums(
        far_tasks(), levels, lefts, lanes, values, col_n, col_s, row_n, row_s, half, unroll
    )
    for start, out, totals in ((start_n, out_n, row_n), (start_s, out_s, row_s)):
        out[0] = start[0]
        for row in range(3):
            out[row + 1] = start[row + 1] + jnp.transpose(totals[row])[:levels]
    for channel, (ref, totals) in enumerate(((col_n, row_n), (col_s, row_s))):
        to_dom[channel, 0] = fold_column(ref, 0, levels)
        to_dom[channel, 1] = fold_column(ref, 1, levels)
        to_slab[channel, 0] = fold_column(ref, 2, levels)
        to_slab[channel, 1] = fold_column(ref, 3, levels) + jnp.transpose(totals[3])[:levels]
        to_edge[channel] = fold_column(ref, 4, levels)


def finish_kernel(raw, own_n, own_s, *refs, levels):
    from_dom, from_slab, from_edge, density, laplace = refs
    for col in range(4):
        sums = []
        for channel, near in enumerate((own_n, own_s)):
            total = near[col]
            if col in (0, 2):
                total = total + from_dom[channel, col // 2]
            if col in (0, 1):
                total = total + from_slab[channel, col]
            if col == 0:
                total = total + from_edge[channel]
            sums.append(total)
        filled = raw[pl.ds(col * levels * 4, levels, 4), :] > 0.5 * far_away
        n = jnp.where(filled, sums[0], 0.0)
        s = jnp.where(filled, sums[1], 0.0)
        f = raw[pl.ds(col * levels * 4 + 3, levels, 4), :]
        density[col] = n / ref_density
        laplace[col] = (s - f * n) / ref_density


def scratch_for(levels, cols, rows):
    span = levels + 2
    f32, bf16 = jnp.float32, jnp.bfloat16
    return [
        pltpu.VMEM((24, levels, 128), f32),
        pltpu.VMEM((4, cols * span, 16, 128), bf16),
        pltpu.VMEM((cols * (levels + 16), 128), f32),
        pltpu.VMEM((rows * levels, 32, 128), bf16),
        pltpu.VMEM((cols * span * 8, 128), f32),
        pltpu.VMEM((cols * span * 8, 128), f32),
        pltpu.VMEM((rows, 128, 128), f32),
        pltpu.VMEM((rows, 128, 128), f32),
    ]


def local(incoming, dest, counts):
    cells_x, cells_y, levels = counts.shape
    slots = incoming.shape[3]
    cells = cells_x * cells_y * levels
    capacity = cells // 4
    slabs, doms = lax.axis_size("slab"), lax.axis_size("dom")
    assert (cells_x, cells_y, slots) == (2, 2, 128) and levels % 8 == 0 and levels <= 128
    assert cells % 128 == 0 and cells <= 16 * 128 and doms >= 5
    assert capacity % 8 == 0 and 128 <= 4 * capacity <= 512
    f32, i32 = jnp.float32, jnp.int32
    shape = jax.ShapeDtypeStruct
    blocks = incoming.reshape(cells, 4, slots)
    *packs, stayed = pl.pallas_call(
        functools.partial(pack_kernel, cells=cells, capacity=capacity, domains=doms),
        out_shape=[shape((capacity + 1, 4, slots), f32)] * 4 + [shape((cells, 4, slots), f32)],
        in_specs=[vmem, vmem],
        out_specs=[vmem] * 5,
        scratch_shapes=[
            pltpu.VMEM((4 * capacity + cells, 4, slots), f32),
            pltpu.VMEM((cells // 128, 128), i32),
            pltpu.SMEM((cells // 128, 128), i32),
            pltpu.SemaphoreType.DMA,
        ],
        compiler_params=params,
        name="pack",
    )(dest.reshape(cells // 128, 128), blocks)
    got = [
        lax.ppermute(pack, "dom", [(i, (i + step) % doms) for i in range(doms)])
        for step, pack in zip(offsets, packs)
    ]
    column = (levels, 4, slots)
    home, to_dom, to_slab, to_edge = pl.pallas_call(
        functools.partial(place_kernel, cells=cells, capacity=capacity, levels=levels),
        out_shape=[shape((cells, 4, slots), f32)]
        + [shape((2 * levels, 4, slots), f32)] * 2
        + [shape(column, f32)],
        in_specs=[vmem] * 5 + [smem],
        out_specs=[vmem] * 4,
        scratch_shapes=[
            pltpu.VMEM((cells + 1, 4, slots), f32),
            pltpu.VMEM((4, 4, 128), i32),
            pltpu.SMEM((4, 4, 128), i32),
            pltpu.SemaphoreType.DMA,
        ],
        compiler_params=params,
        name="place",
    )(*got, stayed, counts)

    both = ("slab", "dom")

    def route(step_slab, step_dom):
        pairs = []
        for s in range(slabs):
            for d in range(doms):
                if 0 <= s + step_slab < slabs and 0 <= d + step_dom < doms:
                    pairs.append((s * doms + d, (s + step_slab) * doms + d + step_dom))
        return pairs

    def send(value, step_slab, step_dom):
        return lax.ppermute(value, both, route(step_slab, step_dom))

    def rows_of(value):
        return value.reshape(-1, slots)

    slab_raw = send(to_slab, -1, 0)
    dom_raw = send(to_dom, 0, -1)
    edge_raw = send(to_edge, -1, -1)
    raw = rows_of(home)
    half = 128
    plane = (4, levels, slots)

    def cost(tiles):
        return pl.CostEstimate(
            flops=levels * tiles * 128 * 128 * 600,
            bytes_accessed=cells * 4 * slots * 4,
            transcendentals=0,
        )

    def own_pairs(first, last, unroll, *start):
        return pl.pallas_call(
            functools.partial(
                own_kernel, levels=levels, half=half, unroll=unroll, first=first, last=last
            ),
            out_shape=[shape(plane, f32)] * 2,
            in_specs=[vmem] * (1 + len(start)),
            out_specs=[vmem] * 2,
            scratch_shapes=scratch_for(levels, 4 - first, last - first),
            compiler_params=params,
            cost_estimate=cost(26),
            name="own",
        )(raw, *start)

    early_n, early_s = own_pairs(0, 1, 4)
    far_n, far_s, ret_dom, ret_slab, ret_edge = pl.pallas_call(
        functools.partial(
            far_kernel, levels=levels, half=half, unroll=4, slabs=slabs, doms=doms
        ),
        out_shape=[shape(plane, f32)] * 2
        + [shape((2, 2, levels, slots), f32)] * 2
        + [shape((2, levels, slots), f32)],
        in_specs=[vmem] * 6,
        out_specs=[vmem] * 5,
        scratch_shapes=scratch_for(levels, 5, 4),
        compiler_params=params,
        cost_estimate=cost(30),
        name="far",
    )(raw, rows_of(dom_raw), rows_of(slab_raw), rows_of(edge_raw), early_n, early_s)
    from_slab = send(ret_slab, 1, 0)
    from_dom = send(ret_dom, 0, 1)
    from_edge = send(ret_edge, 1, 1)
    own_n, own_s = own_pairs(1, 4, 4, far_n, far_s)
    density, laplace = pl.pallas_call(
        functools.partial(finish_kernel, levels=levels),
        out_shape=[shape(plane, f32)] * 2,
        in_specs=[vmem] * 6,
        out_specs=[vmem] * 2,
        compiler_params=params,
        name="finish",
    )(raw, own_n, own_s, from_dom, from_slab, from_edge)
    final = (cells_x, cells_y, levels, slots)
    return density.reshape(final), laplace.reshape(final)


def solution(mesh):
    in_specs = (P("slab", "dom", None, None), P("slab", "dom"), P("slab", "dom", None))
    out_specs = (P("slab", "dom", None, None), P("slab", "dom", None, None))
    return jax.shard_map(local, mesh=mesh, in_specs=in_specs, out_specs=out_specs, check_vma=False)
```

```python
import functools

import jax
import jax.numpy as jnp
from jax import lax
from jax.experimental import pallas as pl
from jax.experimental.pallas import tpu as pltpu
from jax.sharding import PartitionSpec as P

ref_density = 268.0825731
min_square = 0.01
far_away = -1024.0
far_norm = 4096.0
reach = 2
offsets = (-2, -1, 1, 2)

smem = pl.BlockSpec(memory_space=pltpu.SMEM)
vmem = pl.BlockSpec(memory_space=pltpu.VMEM)
params = pltpu.CompilerParams(vmem_limit_bytes=58 * 1024 * 1024)


def pack_kernel(dest, blocks, *refs, cells, capacity, domains):
    outs, home, sorted_blocks, spots, places, sem = refs[:4], *refs[4:9]
    me = lax.axis_index("dom")
    rows = cells // 128
    target = dest[...]
    spot = jnp.zeros((rows, 128), jnp.int32)
    local = jnp.zeros((rows, 128), jnp.int32)
    lane = lax.broadcasted_iota(jnp.int32, (128, 128), 1)
    row = lax.broadcasted_iota(jnp.int32, (128, 128), 0)
    before = jnp.where(row < lane, 1.0, 0.0).astype(jnp.bfloat16)
    whole = jnp.ones((128, 128), jnp.bfloat16)
    for g, step in enumerate(offsets + (0,)):
        owner = lax.rem(me + step + domains, domains)
        within = target - owner * cells
        chosen = jnp.logical_and(within >= 0, within < cells)
        local = jnp.where(chosen, within, local)
        if step == 0:
            rank = within
        else:
            ones = jnp.concatenate(
                [jnp.where(chosen, 1.0, 0.0), jnp.zeros((16 - rows, 128), jnp.float32)], 0
            ).astype(jnp.bfloat16)
            inside = jnp.dot(ones, before, preferred_element_type=jnp.float32)[:rows]
            counted = jnp.dot(ones, whole, preferred_element_type=jnp.float32)[:rows]
            earlier = [jnp.zeros((1, 128), jnp.float32)]
            for r in range(rows - 1):
                earlier.append(earlier[-1] + counted[r : r + 1])
            rank = (inside + jnp.concatenate(earlier, 0)).astype(jnp.int32)
        spot = jnp.where(chosen, g * capacity + rank, spot)
    spots[...] = spot
    copy = pltpu.make_async_copy(spots, places, sem)
    copy.start()
    high = jnp.floor((local + 1).astype(jnp.float32) * (1.0 / 128.0))
    low = (local + 1).astype(jnp.float32) - 128.0 * high
    filler = jnp.zeros((7, 128), jnp.float32)
    sent = 4 * capacity
    marks = [jnp.zeros((8, sent), jnp.float32)] * 2
    slot = lax.broadcasted_iota(jnp.int32, (sent, 128), 0)
    for r in range(rows):
        hit = jnp.where(slot == spot[r : r + 1], 1.0, 0.0).astype(jnp.bfloat16)
        for k, value in enumerate((high, low)):
            marks[k] = marks[k] + lax.dot_general(
                jnp.concatenate([value[r : r + 1], filler], 0).astype(jnp.bfloat16),
                hit,
                (((1,), (1,)), ((), ())),
                preferred_element_type=jnp.float32,
            )
    marks = (128.0 * marks[0] + marks[1])[:1]
    copy.wait()

    def move(k, _):
        for u in range(16):
            b = k * 16 + u
            sorted_blocks[places[b // 128, lax.rem(b, 128)]] = blocks[b]
        return 0

    lax.fori_loop(0, cells // 16, move, 0)
    for g in range(4):
        for k in range(0, capacity, 8):
            outs[g][k : k + 8] = sorted_blocks[g * capacity + k : g * capacity + k + 8]
        for r in range(4):
            at = min(r * 128, sent - 128)
            outs[g][capacity, r : r + 1] = marks[:, at : at + 128]
    home[...] = sorted_blocks[4 * capacity :]


def place_kernel(*refs, cells, capacity, levels):
    got, stayed, counts = refs[:4], refs[4], refs[5]
    home, to_dom, to_slab, to_edge = refs[6:10]
    kept, cell_ids, marks, sem = refs[10:]
    for g in range(4):
        sent = got[g][capacity].astype(jnp.int32) - 1
        cell_ids[g] = jnp.where(sent < 0, cells, sent)
    copy = pltpu.make_async_copy(cell_ids, marks, sem)
    copy.start()
    kept[:cells] = stayed[...]
    copy.wait()
    for g in range(4):

        def put(k, _, g=g):
            for u in range(8):
                slot = k * 8 + u
                spot = g * capacity + slot
                kept[marks[g, spot // 128, lax.rem(spot, 128)]] = got[g][slot]
            return 0

        lax.fori_loop(0, capacity // 8, put, 0)
    lane = lax.broadcasted_iota(jnp.int32, (4, 128), 1)
    row = lax.broadcasted_iota(jnp.int32, (4, 128), 0)
    blank = jnp.where(row == 0, far_away, 0.0)

    def finish(k, _):
        for u in range(4):
            z = k * 4 + u
            for col in range(4):
                cell = col * levels + z
                block = jnp.where(lane < counts[col // 2, col % 2, z], kept[cell], blank)
                home[cell] = block
                if col == 0:
                    to_dom[z] = block
                    to_slab[z] = block
                    to_edge[z] = block
                if col == 1:
                    to_slab[levels + z] = block
                if col == 2:
                    to_dom[levels + z] = block
        return 0

    lax.fori_loop(0, levels // 4, finish, 0)


def split3(value):
    high = value.astype(jnp.bfloat16).astype(jnp.float32)
    rest = value - high
    mid = rest.astype(jnp.bfloat16).astype(jnp.float32)
    return high, mid, rest - mid


def load_points(raw, first, corner_x, corner_y, level, valid):
    x = raw[pl.ds(first, 8, 4), :]
    y = raw[pl.ds(first + 1, 8, 4), :]
    z = raw[pl.ds(first + 2, 8, 4), :]
    f = raw[pl.ds(first + 3, 8, 4), :]
    if valid is not None:
        x = jnp.where(valid, x, far_away)
        f = jnp.where(valid, f, 0.0)
    rows = lax.broadcasted_iota(jnp.int32, (8, 128), 0) + level
    return x - corner_x, y - corner_y, z - (rows.astype(jnp.float32) + 0.5), f


def make_lanes(raw, base, col, levels, corner_x, corner_y, valid, parts, lanes, values):
    span = levels + 2
    rows = lax.broadcasted_iota(jnp.int32, (8, 128), 0)
    zero = jnp.zeros((8, 128), jnp.float32)

    def chunk(k, _):
        level = pl.multiple_of(k * 8, 8)
        first = pl.multiple_of((base + level) * 4, 32)
        x, y, z, f = load_points(raw, first, corner_x, corner_y, level, valid)
        values[pl.ds(pl.multiple_of(col * (levels + 16) + 8 + level, 8), 8), :] = f
        found = [*split3(x), *split3(y)]
        flat_norm = x * x + y * y
        for shift in range(3):
            moved = z + float(shift - 1)
            found += [*split3(moved), *split3(flat_norm + moved * moved)]
        for p, value in enumerate(found):
            parts[p, pl.ds(level, 8), :] = value
        return 0

    lax.fori_loop(0, levels // 8, chunk, 0)
    rows16 = lax.broadcasted_iota(jnp.int32, (16, 128), 0)
    empty = jnp.where(rows16 == 6, far_norm, 0.0).astype(jnp.bfloat16)
    for edge in (0, levels + 1):
        lanes[0, col * span + edge] = jnp.zeros((16, 128), jnp.bfloat16)
        for shift in range(3):
            lanes[1 + shift, col * span + edge] = empty
    values[pl.ds(col * (levels + 16), 8), :] = zero
    values[pl.ds(col * (levels + 16) + 8 + levels, 8), :] = zero

    def is_in(*which):
        return functools.reduce(jnp.logical_or, [rows == r for r in which])

    mids, low, third, head = is_in(1, 3, 7), is_in(4), is_in(2), is_in(0)
    tail = rows >= 6
    units = jnp.where(rows < 7, 1.0, 0.0)

    def narrow(k, _):
        for u in range(4):
            z = k * 4 + u

            def part(p, z=z):
                return jnp.broadcast_to(parts[p, pl.ds(z, 1), :], (8, 128))

            def six(first, then):
                high = jnp.where(tail, part(then), part(first))
                mid = jnp.where(tail, part(then + 1), part(first + 1))
                return jnp.where(mids, mid, jnp.where(low, part(first + 2), high))

            upper = six(0, 3)
            lower = jnp.where(is_in(1), part(4), jnp.where(third, part(5), part(3)))
            lower = jnp.where(rows >= 4, units, lower)
            at = col * span + 1 + z
            lanes[0, at] = jnp.concatenate([upper, lower], 0).astype(jnp.bfloat16)
            for shift in range(3):
                p = 6 + shift * 6
                upper = six(p, p + 3)
                lower = jnp.where(head, part(p + 5), zero)
                lanes[1 + shift, at] = jnp.concatenate([upper, lower], 0).astype(jnp.bfloat16)
        return 0

    lax.fori_loop(0, levels // 4, narrow, 0)


def make_rows(raw, base, row, levels, corner_x, corner_y, valid, parts, lefts):
    rows = lax.broadcasted_iota(jnp.int32, (8, 128), 0)

    def chunk(k, _):
        level = pl.multiple_of(k * 8, 8)
        first = pl.multiple_of((base + level) * 4, 32)
        x, y, z, f = load_points(raw, first, corner_x, corner_y, level, valid)
        found = []
        for value in (x, y, z):
            found += [-2.0 * part for part in split3(value)]
        found += [*split3(x * x + y * y + z * z), *split3(f)]
        for p, value in enumerate(found):
            parts[p, pl.ds(level, 8), :] = value
        return 0

    lax.fori_loop(0, levels // 8, chunk, 0)

    def pick(choices):
        value = choices[-1][1]
        for which, other in choices[:-1]:
            hit = functools.reduce(jnp.logical_or, [rows == r for r in which])
            value = jnp.where(hit, other, value)
        return value

    def narrow(k, _):
        for u in range(4):
            z = k * 4 + u

            def part(p, z=z):
                return jnp.broadcast_to(parts[p, pl.ds(z, 1), :], (8, 128))

            tile = [
                pick([((2, 3), part(1)), ((5,), part(2)), ((6, 7), part(3)), ((), part(0))]),
                pick(
                    [
                        ((0, 1), part(4)),
                        ((2,), part(3)),
                        ((3,), part(5)),
                        ((4,), part(9)),
                        ((5,), part(10)),
                        ((6,), part(11)),
                        ((), jnp.zeros((8, 128), jnp.float32)),
                    ]
                ),
                pick(
                    [
                        ((2, 3), part(7)),
                        ((5,), part(8)),
                        ((6, 7), jnp.ones((8, 128), jnp.float32)),
                        ((), part(6)),
                    ]
                ),
                pick(
                    [
                        ((1,), part(12)),
                        ((2,), part(13)),
                        ((3,), part(14)),
                        ((), jnp.where(rows == 0, 1.0, 0.0)),
                    ]
                ),
            ]
            lefts[row * levels + z] = jnp.concatenate(tile, 0).astype(jnp.bfloat16)
        return 0

    lax.fori_loop(0, levels // 4, narrow, 0)


def pair_sums(
    tasks, levels, lefts, lanes, values, col_n, col_s, row_n, row_s, half, unroll
):
    span = levels + 2
    row_n[...] = jnp.zeros_like(row_n)
    row_s[...] = jnp.zeros_like(row_s)
    col_n[...] = jnp.zeros_like(col_n)
    col_s[...] = jnp.zeros_like(col_s)
    groups = half // 8
    spots = lax.broadcasted_iota(jnp.int32, (32, 128), 0)
    picks = jnp.logical_and(spots >= 25, spots < 28)
    field_rows = jnp.where(picks, 1.0, 0.0).astype(jnp.bfloat16)

    def right(z, tile):
        if tile is None:
            return field_rows
        col, shift, _ = tile
        at = col * span + 1 + z + shift
        return jnp.concatenate([lanes[0, at], lanes[2 + shift, at]], axis=0)

    def weights(square):
        return lax.rsqrt(jnp.minimum(jnp.maximum(square, min_square), 1.0))

    def level_step(z):
        mine = lax.broadcasted_iota(jnp.int32, (8, 128), 1) == z
        for row, tiles in tasks:
            total = None
            fields = {}
            for tile in tiles:
                col, shift, _ = tile
                f = values[pl.ds(col * (levels + 16) + 8 + z + shift, 1), :]
                fields[tile] = f
                total = f if total is None else total + f
            queue = [None] + tiles
            whole = jnp.transpose(lefts[row * levels + z])
            for part in range(128 // half):
                left = whole[part * half : (part + 1) * half]
                sums_n = [jnp.full((8, 128), -float(len(tiles)), jnp.float32)] * groups
                sums_s = [jnp.broadcast_to(-total, (8, 128))] * groups
                own = own_sum = None
                for t in range(0, len(queue), 2):
                    pair = queue[t : t + 2]
                    rights = [right(z, tile) for tile in pair]
                    square = lax.dot_general(
                        left,
                        jnp.concatenate(rights, axis=1) if len(pair) == 2 else rights[0],
                        (((1,), (0,)), ((), ())),
                        preferred_element_type=jnp.float32,
                    )
                    for p, tile in enumerate(pair):
                        pieces = [
                            square[g * 8 : g * 8 + 8, p * 128 : p * 128 + 128]
                            for g in range(groups)
                        ]
                        if tile is None:
                            own = pieces
                            own_sum = functools.reduce(jnp.add, own)
                            continue
                        col, shift, both = tile
                        f = fields[tile]
                        down_n = jnp.full((8, 128), -float(groups), jnp.float32)
                        down_s = -own_sum
                        for g in range(groups):
                            w = weights(pieces[g])
                            sums_n[g] = sums_n[g] + w
                            sums_s[g] = sums_s[g] + w * f
                            if both:
                                down_n = down_n + w
                                down_s = down_s + w * own[g]
                        if both:
                            at = pl.ds(pl.multiple_of((col * span + 1 + z + shift) * 8, 8), 8)
                            col_n[at, :] += down_n
                            col_s[at, :] += down_s
                for totals, sums in ((row_n, sums_n), (row_s, sums_s)):
                    for g in range(groups):
                        at = slice(part * half + g * 8, part * half + g * 8 + 8)
                        totals[row, at, :] = jnp.where(
                            mine, jnp.sum(sums[g], axis=1, keepdims=True), totals[row, at, :]
                        )

    def some_levels(k, _):
        for u in range(unroll):
            level_step(k * unroll + u)
        return 0

    lax.fori_loop(0, levels // unroll, some_levels, 0)


def fold_column(ref, col, levels):
    base = (col * (levels + 2) + 1) * 8
    total = None
    for k in range(8):
        part = ref[pl.ds(base + k, levels, 8), :]
        total = part if total is None else total + part
    return total


def own_tasks(rows):
    tasks = []
    for row in rows:
        tiles = [(row, 0, False), (row, 1, True)]
        for col in range(row + 1, 4):
            tiles += [(col, shift, True) for shift in (-1, 0, 1)]
        tasks.append((row, tiles))
    return tasks


def far_tasks():
    wanted = ((0, (0, 1)), (1, (2, 3)), (2, (0, 1, 2, 3, 4)), (3, (1,)))
    return [
        (row, [(col, shift, True) for col in cols for shift in (-1, 0, 1)])
        for row, cols in wanted
    ]


def corners():
    corner_x = (lax.axis_index("slab") * 2 + 1).astype(jnp.float32)
    corner_y = (lax.axis_index("dom") * 2 + 1).astype(jnp.float32)
    return corner_x, corner_y


def own_kernel(raw, *refs, levels, half, unroll, first, last):
    count = 4 - first
    starts, refs = (refs[:2], refs[2:]) if first else (None, refs)
    (out_n, out_s), scratch = refs[:2], refs[2:]
    parts, lanes, values, lefts, col_n, col_s, row_n, row_s = scratch
    corner_x, corner_y = corners()
    for col in range(count):
        base = (col + first) * levels
        make_lanes(raw, base, col, levels, corner_x, corner_y, None, parts, lanes, values)
    for row in range(last - first):
        make_rows(
            raw, (row + first) * levels, row, levels, corner_x, corner_y, None, parts, lefts
        )
    tasks = [
        (row - first, [(col - first, shift, both) for col, shift, both in tiles])
        for row, tiles in own_tasks(range(first, last))
    ]
    pair_sums(tasks, levels, lefts, lanes, values, col_n, col_s, row_n, row_s, half, unroll)
    for col in range(4):
        if col < first:
            out_n[col] = starts[0][col]
            out_s[col] = starts[1][col]
            continue
        n = fold_column(col_n, col - first, levels)
        s = fold_column(col_s, col - first, levels)
        if col < last:
            f = values[pl.ds((col - first) * (levels + 16) + 8, levels), :]
            itself = lax.rsqrt(jnp.maximum(0.0 * f, min_square)) - 1.0
            n = n + jnp.transpose(row_n[col - first])[:levels] - itself
            s = s + jnp.transpose(row_s[col - first])[:levels] - itself * f
        if first:
            n = n + starts[0][col]
            s = s + starts[1][col]
        out_n[col] = n
        out_s[col] = s


def far_kernel(raw, dom_raw, slab_raw, edge_raw, *refs, levels, half, unroll, slabs, doms):
    start_n, start_s, out_n, out_s, to_dom, to_slab, to_edge = refs[:7]
    parts, lanes, values, lefts, col_n, col_s, row_n, row_s = refs[7:]
    corner_x, corner_y = corners()
    next_slab = lax.axis_index("slab") + 1 < slabs
    next_dom = lax.axis_index("dom") + 1 < doms
    sources = (
        (dom_raw, 0, next_dom),
        (dom_raw, levels, next_dom),
        (slab_raw, 0, next_slab),
        (slab_raw, levels, next_slab),
        (edge_raw, 0, jnp.logical_and(next_slab, next_dom)),
    )
    for col, (source, base, valid) in enumerate(sources):
        make_lanes(source, base, col, levels, corner_x, corner_y, valid, parts, lanes, values)
    for row in range(3):
        make_rows(raw, (row + 1) * levels, row, levels, corner_x, corner_y, None, parts, lefts)
    make_rows(slab_raw, levels, 3, levels, corner_x, corner_y, next_slab, parts, lefts)
    pair_sums(
        far_tasks(), levels, lefts, lanes, values, col_n, col_s, row_n, row_s, half, unroll
    )
    for start, out, totals in ((start_n, out_n, row_n), (start_s, out_s, row_s)):
        out[0] = start[0]
        for row in range(3):
            out[row + 1] = start[row + 1] + jnp.transpose(totals[row])[:levels]
    for channel, (ref, totals) in enumerate(((col_n, row_n), (col_s, row_s))):
        for k in range(2):
            to_dom[channel, k] = jnp.where(next_dom, fold_column(ref, k, levels), 0.0)
        near = fold_column(ref, 2, levels)
        to_slab[channel, 0] = jnp.where(next_slab, near, 0.0)
        near = fold_column(ref, 3, levels) + jnp.transpose(totals[3])[:levels]
        to_slab[channel, 1] = jnp.where(next_slab, near, 0.0)
        near = fold_column(ref, 4, levels)
        to_edge[channel] = jnp.where(jnp.logical_and(next_slab, next_dom), near, 0.0)


def finish_kernel(raw, own_n, own_s, *refs, levels):
    from_dom, from_slab, from_edge, density, laplace = refs
    for col in range(4):
        sums = []
        for channel, near in enumerate((own_n, own_s)):
            total = near[col]
            if col in (0, 2):
                total = total + from_dom[channel, col // 2]
            if col in (0, 1):
                total = total + from_slab[channel, col]
            if col == 0:
                total = total + from_edge[channel]
            sums.append(total)
        filled = raw[pl.ds(col * levels * 4, levels, 4), :] > 0.5 * far_away
        n = jnp.where(filled, sums[0], 0.0)
        s = jnp.where(filled, sums[1], 0.0)
        f = raw[pl.ds(col * levels * 4 + 3, levels, 4), :]
        density[col] = n / ref_density
        laplace[col] = (s - f * n) / ref_density


def scratch_for(levels, cols, rows):
    span = levels + 2
    f32, bf16 = jnp.float32, jnp.bfloat16
    return [
        pltpu.VMEM((24, levels, 128), f32),
        pltpu.VMEM((4, cols * span, 16, 128), bf16),
        pltpu.VMEM((cols * (levels + 16), 128), f32),
        pltpu.VMEM((rows * levels, 32, 128), bf16),
        pltpu.VMEM((cols * span * 8, 128), f32),
        pltpu.VMEM((cols * span * 8, 128), f32),
        pltpu.VMEM((rows, 128, 128), f32),
        pltpu.VMEM((rows, 128, 128), f32),
    ]


def local(incoming, dest, counts):
    cells_x, cells_y, levels = counts.shape
    slots = incoming.shape[3]
    cells = cells_x * cells_y * levels
    capacity = cells // 4
    slabs, doms = lax.axis_size("slab"), lax.axis_size("dom")
    assert (cells_x, cells_y, slots) == (2, 2, 128) and levels % 8 == 0 and levels <= 128
    assert cells % 128 == 0 and cells <= 16 * 128 and doms >= 5
    assert capacity % 8 == 0 and 128 <= 4 * capacity <= 512
    f32, i32 = jnp.float32, jnp.int32
    shape = jax.ShapeDtypeStruct
    blocks = incoming.reshape(cells, 4, slots)
    *packs, stayed = pl.pallas_call(
        functools.partial(pack_kernel, cells=cells, capacity=capacity, domains=doms),
        out_shape=[shape((capacity + 1, 4, slots), f32)] * 4 + [shape((cells, 4, slots), f32)],
        in_specs=[vmem, vmem],
        out_specs=[vmem] * 5,
        scratch_shapes=[
            pltpu.VMEM((4 * capacity + cells, 4, slots), f32),
            pltpu.VMEM((cells // 128, 128), i32),
            pltpu.SMEM((cells // 128, 128), i32),
            pltpu.SemaphoreType.DMA,
        ],
        compiler_params=params,
        name="pack",
    )(dest.reshape(cells // 128, 128), blocks)
    got = [
        lax.ppermute(pack, "dom", [(i, (i + step) % doms) for i in range(doms)])
        for step, pack in zip(offsets, packs)
    ]
    column = (levels, 4, slots)
    home, to_dom, to_slab, to_edge = pl.pallas_call(
        functools.partial(place_kernel, cells=cells, capacity=capacity, levels=levels),
        out_shape=[shape((cells, 4, slots), f32)]
        + [shape((2 * levels, 4, slots), f32)] * 2
        + [shape(column, f32)],
        in_specs=[vmem] * 5 + [smem],
        out_specs=[vmem] * 4,
        scratch_shapes=[
            pltpu.VMEM((cells + 1, 4, slots), f32),
            pltpu.VMEM((4, 4, 128), i32),
            pltpu.SMEM((4, 4, 128), i32),
            pltpu.SemaphoreType.DMA,
        ],
        compiler_params=params,
        name="place",
    )(*got, stayed, counts)

    both = ("slab", "dom")

    def route(step_slab, step_dom):
        return [
            (s * doms + d, (s + step_slab) % slabs * doms + (d + step_dom) % doms)
            for s in range(slabs)
            for d in range(doms)
        ]

    def send(value, step_slab, step_dom):
        return lax.ppermute(value, both, route(step_slab, step_dom))

    def rows_of(value):
        return value.reshape(-1, slots)

    slab_raw = send(to_slab, -1, 0)
    dom_raw = send(to_dom, 0, -1)
    edge_raw = send(to_edge, -1, -1)
    raw = rows_of(home)
    half = 128
    plane = (4, levels, slots)

    def cost(tiles):
        return pl.CostEstimate(
            flops=levels * tiles * 128 * 128 * 600,
            bytes_accessed=cells * 4 * slots * 4,
            transcendentals=0,
        )

    def own_pairs(first, last, unroll, *start):
        return pl.pallas_call(
            functools.partial(
                own_kernel, levels=levels, half=half, unroll=unroll, first=first, last=last
            ),
            out_shape=[shape(plane, f32)] * 2,
            in_specs=[vmem] * (1 + len(start)),
            out_specs=[vmem] * 2,
            scratch_shapes=scratch_for(levels, 4 - first, last - first),
            compiler_params=params,
            cost_estimate=cost(26),
            name="own",
        )(raw, *start)

    early_n, early_s = own_pairs(0, 1, 4)
    far_n, far_s, ret_dom, ret_slab, ret_edge = pl.pallas_call(
        functools.partial(
            far_kernel, levels=levels, half=half, unroll=4, slabs=slabs, doms=doms
        ),
        out_shape=[shape(plane, f32)] * 2
        + [shape((2, 2, levels, slots), f32)] * 2
        + [shape((2, levels, slots), f32)],
        in_specs=[vmem] * 6,
        out_specs=[vmem] * 5,
        scratch_shapes=scratch_for(levels, 5, 4),
        compiler_params=params,
        cost_estimate=cost(30),
        name="far",
    )(raw, rows_of(dom_raw), rows_of(slab_raw), rows_of(edge_raw), early_n, early_s)
    from_slab = send(ret_slab, 1, 0)
    from_dom = send(ret_dom, 0, 1)
    from_edge = send(ret_edge, 1, 1)
    own_n, own_s = own_pairs(1, 4, 4, far_n, far_s)
    density, laplace = pl.pallas_call(
        functools.partial(finish_kernel, levels=levels),
        out_shape=[shape(plane, f32)] * 2,
        in_specs=[vmem] * 6,
        out_specs=[vmem] * 2,
        compiler_params=params,
        name="finish",
    )(raw, own_n, own_s, from_dom, from_slab, from_edge)
    final = (cells_x, cells_y, levels, slots)
    return density.reshape(final), laplace.reshape(final)


def solution(mesh):
    in_specs = (P("slab", "dom", None, None), P("slab", "dom"), P("slab", "dom", None))
    out_specs = (P("slab", "dom", None, None), P("slab", "dom", None, None))
    return jax.shard_map(local, mesh=mesh, in_specs=in_specs, out_specs=out_specs, check_vma=False)
```

```python
import functools

import jax
import jax.numpy as jnp
from jax import lax
from jax.experimental import pallas as pl
from jax.experimental.pallas import tpu as pltpu
from jax.sharding import PartitionSpec as P

ref_density = 268.0825731
min_square = 0.01
far_away = -1024.0
far_norm = 4096.0
reach = 2
offsets = (-2, -1, 1, 2)

smem = pl.BlockSpec(memory_space=pltpu.SMEM)
vmem = pl.BlockSpec(memory_space=pltpu.VMEM)
params = pltpu.CompilerParams(vmem_limit_bytes=58 * 1024 * 1024)


def pack_kernel(dest, blocks, *refs, cells, capacity, domains):
    outs, home, sorted_blocks, spots, places, sem = refs[:4], *refs[4:9]
    me = lax.axis_index("dom")
    rows = cells // 128
    target = dest[...]
    spot = jnp.zeros((rows, 128), jnp.int32)
    local = jnp.zeros((rows, 128), jnp.int32)
    lane = lax.broadcasted_iota(jnp.int32, (128, 128), 1)
    row = lax.broadcasted_iota(jnp.int32, (128, 128), 0)
    before = jnp.where(row < lane, 1.0, 0.0).astype(jnp.bfloat16)
    whole = jnp.ones((128, 128), jnp.bfloat16)
    for g, step in enumerate(offsets + (0,)):
        owner = lax.rem(me + step + domains, domains)
        within = target - owner * cells
        chosen = jnp.logical_and(within >= 0, within < cells)
        local = jnp.where(chosen, within, local)
        if step == 0:
            rank = within
        else:
            ones = jnp.concatenate(
                [jnp.where(chosen, 1.0, 0.0), jnp.zeros((16 - rows, 128), jnp.float32)], 0
            ).astype(jnp.bfloat16)
            inside = jnp.dot(ones, before, preferred_element_type=jnp.float32)[:rows]
            counted = jnp.dot(ones, whole, preferred_element_type=jnp.float32)[:rows]
            earlier = [jnp.zeros((1, 128), jnp.float32)]
            for r in range(rows - 1):
                earlier.append(earlier[-1] + counted[r : r + 1])
            rank = (inside + jnp.concatenate(earlier, 0)).astype(jnp.int32)
        spot = jnp.where(chosen, g * capacity + rank, spot)
    spots[...] = spot
    copy = pltpu.make_async_copy(spots, places, sem)
    copy.start()
    high = jnp.floor((local + 1).astype(jnp.float32) * (1.0 / 128.0))
    low = (local + 1).astype(jnp.float32) - 128.0 * high
    filler = jnp.zeros((7, 128), jnp.float32)
    sent = 4 * capacity
    marks = [jnp.zeros((8, sent), jnp.float32)] * 2
    slot = lax.broadcasted_iota(jnp.int32, (sent, 128), 0)
    for r in range(rows):
        hit = jnp.where(slot == spot[r : r + 1], 1.0, 0.0).astype(jnp.bfloat16)
        for k, value in enumerate((high, low)):
            marks[k] = marks[k] + lax.dot_general(
                jnp.concatenate([value[r : r + 1], filler], 0).astype(jnp.bfloat16),
                hit,
                (((1,), (1,)), ((), ())),
                preferred_element_type=jnp.float32,
            )
    marks = (128.0 * marks[0] + marks[1])[:1]
    copy.wait()

    def move(k, _):
        for u in range(16):
            b = k * 16 + u
            sorted_blocks[places[b // 128, lax.rem(b, 128)]] = blocks[b]
        return 0

    lax.fori_loop(0, cells // 16, move, 0)
    for g in range(4):
        for k in range(0, capacity, 8):
            outs[g][k : k + 8] = sorted_blocks[g * capacity + k : g * capacity + k + 8]
        for r in range(4):
            at = min(r * 128, sent - 128)
            outs[g][capacity, r : r + 1] = marks[:, at : at + 128]
    home[...] = sorted_blocks[4 * capacity :]


def place_kernel(*refs, cells, capacity, levels):
    got, stayed, counts = refs[:4], refs[4], refs[5]
    home, to_dom, to_slab, to_edge = refs[6:10]
    kept, cell_ids, marks, sem = refs[10:]
    for g in range(4):
        sent = got[g][capacity].astype(jnp.int32) - 1
        cell_ids[g] = jnp.where(sent < 0, cells, sent)
    copy = pltpu.make_async_copy(cell_ids, marks, sem)
    copy.start()
    kept[:cells] = stayed[...]
    copy.wait()
    for g in range(4):

        def put(k, _, g=g):
            for u in range(8):
                slot = k * 8 + u
                spot = g * capacity + slot
                kept[marks[g, spot // 128, lax.rem(spot, 128)]] = got[g][slot]
            return 0

        lax.fori_loop(0, capacity // 8, put, 0)
    lane = lax.broadcasted_iota(jnp.int32, (4, 128), 1)
    row = lax.broadcasted_iota(jnp.int32, (4, 128), 0)
    blank = jnp.where(row == 0, far_away, 0.0)

    def finish(k, _):
        for u in range(4):
            z = k * 4 + u
            for col in range(4):
                cell = col * levels + z
                block = jnp.where(lane < counts[col // 2, col % 2, z], kept[cell], blank)
                home[cell] = block
                if col == 0:
                    to_dom[z] = block
                    to_slab[z] = block
                    to_edge[z] = block
                if col == 1:
                    to_slab[levels + z] = block
                if col == 2:
                    to_dom[levels + z] = block
        return 0

    lax.fori_loop(0, levels // 4, finish, 0)


def split3(value):
    high = value.astype(jnp.bfloat16).astype(jnp.float32)
    rest = value - high
    mid = rest.astype(jnp.bfloat16).astype(jnp.float32)
    return high, mid, rest - mid


def load_points(raw, first, corner_x, corner_y, level, valid):
    x = raw[pl.ds(first, 8, 4), :]
    y = raw[pl.ds(first + 1, 8, 4), :]
    z = raw[pl.ds(first + 2, 8, 4), :]
    f = raw[pl.ds(first + 3, 8, 4), :]
    if valid is not None:
        x = jnp.where(valid, x, far_away)
        f = jnp.where(valid, f, 0.0)
    rows = lax.broadcasted_iota(jnp.int32, (8, 128), 0) + level
    return x - corner_x, y - corner_y, z - (rows.astype(jnp.float32) + 0.5), f


def make_lanes(raw, base, col, levels, corner_x, corner_y, valid, parts, lanes, values):
    span = levels + 2
    rows = lax.broadcasted_iota(jnp.int32, (8, 128), 0)
    zero = jnp.zeros((8, 128), jnp.float32)

    def chunk(k, _):
        level = pl.multiple_of(k * 8, 8)
        first = pl.multiple_of((base + level) * 4, 32)
        x, y, z, f = load_points(raw, first, corner_x, corner_y, level, valid)
        values[pl.ds(pl.multiple_of(col * (levels + 16) + 8 + level, 8), 8), :] = f
        found = [*split3(x), *split3(y)]
        flat_norm = x * x + y * y
        for shift in range(3):
            moved = z + float(shift - 1)
            found += [*split3(moved), *split3(flat_norm + moved * moved)]
        for p, value in enumerate(found):
            parts[p, pl.ds(level, 8), :] = value
        return 0

    lax.fori_loop(0, levels // 8, chunk, 0)
    rows16 = lax.broadcasted_iota(jnp.int32, (16, 128), 0)
    empty = jnp.where(rows16 == 6, far_norm, 0.0).astype(jnp.bfloat16)
    for edge in (0, levels + 1):
        lanes[0, col * span + edge] = jnp.zeros((16, 128), jnp.bfloat16)
        for shift in range(3):
            lanes[1 + shift, col * span + edge] = empty
    values[pl.ds(col * (levels + 16), 8), :] = zero
    values[pl.ds(col * (levels + 16) + 8 + levels, 8), :] = zero

    def is_in(*which):
        return functools.reduce(jnp.logical_or, [rows == r for r in which])

    mids, low, third, head = is_in(1, 3, 7), is_in(4), is_in(2), is_in(0)
    tail = rows >= 6
    units = jnp.where(rows < 7, 1.0, 0.0)

    def narrow(k, _):
        for u in range(4):
            z = k * 4 + u

            def part(p, z=z):
                return jnp.broadcast_to(parts[p, pl.ds(z, 1), :], (8, 128))

            def six(first, then):
                high = jnp.where(tail, part(then), part(first))
                mid = jnp.where(tail, part(then + 1), part(first + 1))
                return jnp.where(mids, mid, jnp.where(low, part(first + 2), high))

            upper = six(0, 3)
            lower = jnp.where(is_in(1), part(4), jnp.where(third, part(5), part(3)))
            lower = jnp.where(rows >= 4, units, lower)
            at = col * span + 1 + z
            lanes[0, at] = jnp.concatenate([upper, lower], 0).astype(jnp.bfloat16)
            for shift in range(3):
                p = 6 + shift * 6
                upper = six(p, p + 3)
                lower = jnp.where(head, part(p + 5), zero)
                lanes[1 + shift, at] = jnp.concatenate([upper, lower], 0).astype(jnp.bfloat16)
        return 0

    lax.fori_loop(0, levels // 4, narrow, 0)


def make_rows(raw, base, row, levels, corner_x, corner_y, valid, parts, lefts):
    rows = lax.broadcasted_iota(jnp.int32, (8, 128), 0)

    def chunk(k, _):
        level = pl.multiple_of(k * 8, 8)
        first = pl.multiple_of((base + level) * 4, 32)
        x, y, z, f = load_points(raw, first, corner_x, corner_y, level, valid)
        found = []
        for value in (x, y, z):
            found += [-2.0 * part for part in split3(value)]
        found += [*split3(x * x + y * y + z * z), *split3(f)]
        for p, value in enumerate(found):
            parts[p, pl.ds(level, 8), :] = value
        return 0

    lax.fori_loop(0, levels // 8, chunk, 0)

    def pick(choices):
        value = choices[-1][1]
        for which, other in choices[:-1]:
            hit = functools.reduce(jnp.logical_or, [rows == r for r in which])
            value = jnp.where(hit, other, value)
        return value

    def narrow(k, _):
        for u in range(4):
            z = k * 4 + u

            def part(p, z=z):
                return jnp.broadcast_to(parts[p, pl.ds(z, 1), :], (8, 128))

            tile = [
                pick([((2, 3), part(1)), ((5,), part(2)), ((6, 7), part(3)), ((), part(0))]),
                pick(
                    [
                        ((0, 1), part(4)),
                        ((2,), part(3)),
                        ((3,), part(5)),
                        ((4,), part(9)),
                        ((5,), part(10)),
                        ((6,), part(11)),
                        ((), jnp.zeros((8, 128), jnp.float32)),
                    ]
                ),
                pick(
                    [
                        ((2, 3), part(7)),
                        ((5,), part(8)),
                        ((6, 7), jnp.ones((8, 128), jnp.float32)),
                        ((), part(6)),
                    ]
                ),
                pick(
                    [
                        ((1,), part(12)),
                        ((2,), part(13)),
                        ((3,), part(14)),
                        ((), jnp.where(rows == 0, 1.0, 0.0)),
                    ]
                ),
            ]
            lefts[row * levels + z] = jnp.concatenate(tile, 0).astype(jnp.bfloat16)
        return 0

    lax.fori_loop(0, levels // 4, narrow, 0)


def pair_sums(
    tasks, levels, lefts, lanes, values, col_n, col_s, row_n, row_s, half, unroll
):
    span = levels + 2
    row_n[...] = jnp.zeros_like(row_n)
    row_s[...] = jnp.zeros_like(row_s)
    col_n[...] = jnp.zeros_like(col_n)
    col_s[...] = jnp.zeros_like(col_s)
    groups = half // 8
    spots = lax.broadcasted_iota(jnp.int32, (32, 128), 0)
    picks = jnp.logical_and(spots >= 25, spots < 28)
    field_rows = jnp.where(picks, 1.0, 0.0).astype(jnp.bfloat16)

    def right(z, tile):
        if tile is None:
            return field_rows
        col, shift, _ = tile
        at = col * span + 1 + z + shift
        return jnp.concatenate([lanes[0, at], lanes[2 + shift, at]], axis=0)

    def weights(square):
        return lax.rsqrt(jnp.minimum(jnp.maximum(square, min_square), 1.0))

    def level_step(z):
        found = {}
        for row, tiles in tasks:
            total = None
            fields = {}
            for tile in tiles:
                col, shift, _ = tile
                f = values[pl.ds(col * (levels + 16) + 8 + z + shift, 1), :]
                fields[tile] = f
                total = f if total is None else total + f
            queue = [None] + tiles
            whole = jnp.transpose(lefts[row * levels + z])
            for part in range(128 // half):
                left = whole[part * half : (part + 1) * half]
                sums_n = [jnp.full((8, 128), -float(len(tiles)), jnp.float32)] * groups
                sums_s = [jnp.broadcast_to(-total, (8, 128))] * groups
                own = own_sum = None
                for t in range(0, len(queue), 2):
                    pair = queue[t : t + 2]
                    rights = [right(z, tile) for tile in pair]
                    square = lax.dot_general(
                        left,
                        jnp.concatenate(rights, axis=1) if len(pair) == 2 else rights[0],
                        (((1,), (0,)), ((), ())),
                        preferred_element_type=jnp.float32,
                    )
                    for p, tile in enumerate(pair):
                        pieces = [
                            square[g * 8 : g * 8 + 8, p * 128 : p * 128 + 128]
                            for g in range(groups)
                        ]
                        if tile is None:
                            own = pieces
                            own_sum = functools.reduce(jnp.add, own)
                            continue
                        col, shift, both = tile
                        f = fields[tile]
                        down_n = jnp.full((8, 128), -float(groups), jnp.float32)
                        down_s = -own_sum
                        for g in range(groups):
                            w = weights(pieces[g])
                            sums_n[g] = sums_n[g] + w
                            sums_s[g] = sums_s[g] + w * f
                            if both:
                                down_n = down_n + w
                                down_s = down_s + w * own[g]
                        if both:
                            at = pl.ds(pl.multiple_of((col * span + 1 + z + shift) * 8, 8), 8)
                            col_n[at, :] += down_n
                            col_s[at, :] += down_s
                for channel, sums in enumerate((sums_n, sums_s)):
                    for g in range(groups):
                        found[channel, row, part * groups + g] = jnp.sum(
                            sums[g], axis=1, keepdims=True
                        )
        return found

    def some_levels(k, _):
        lane = lax.broadcasted_iota(jnp.int32, (8, 128), 1)
        levels_found = [level_step(k * unroll + u) for u in range(unroll)]
        for channel, row, g in levels_found[0]:
            totals = (row_n, row_s)[channel]
            value = totals[row, g * 8 : g * 8 + 8, :]
            for u, found in enumerate(levels_found):
                value = jnp.where(lane == k * unroll + u, found[channel, row, g], value)
            totals[row, g * 8 : g * 8 + 8, :] = value
        return 0

    lax.fori_loop(0, levels // unroll, some_levels, 0)


def fold_column(ref, col, levels):
    base = (col * (levels + 2) + 1) * 8
    total = None
    for k in range(8):
        part = ref[pl.ds(base + k, levels, 8), :]
        total = part if total is None else total + part
    return total


def own_tasks(rows):
    tasks = []
    for row in rows:
        tiles = [(row, 0, False), (row, 1, True)]
        for col in range(row + 1, 4):
            tiles += [(col, shift, True) for shift in (-1, 0, 1)]
        tasks.append((row, tiles))
    return tasks


def far_tasks():
    wanted = ((0, (0, 1)), (1, (2, 3)), (2, (0, 1, 2, 3, 4)), (3, (1,)))
    return [
        (row, [(col, shift, True) for col in cols for shift in (-1, 0, 1)])
        for row, cols in wanted
    ]


def corners():
    corner_x = (lax.axis_index("slab") * 2 + 1).astype(jnp.float32)
    corner_y = (lax.axis_index("dom") * 2 + 1).astype(jnp.float32)
    return corner_x, corner_y


def own_kernel(raw, *refs, levels, half, unroll, first, last):
    count = 4 - first
    starts, refs = (refs[:2], refs[2:]) if first else (None, refs)
    (out_n, out_s), scratch = refs[:2], refs[2:]
    parts, lanes, values, lefts, col_n, col_s, row_n, row_s = scratch
    corner_x, corner_y = corners()
    for col in range(count):
        base = (col + first) * levels
        make_lanes(raw, base, col, levels, corner_x, corner_y, None, parts, lanes, values)
    for row in range(last - first):
        make_rows(
            raw, (row + first) * levels, row, levels, corner_x, corner_y, None, parts, lefts
        )
    tasks = [
        (row - first, [(col - first, shift, both) for col, shift, both in tiles])
        for row, tiles in own_tasks(range(first, last))
    ]
    pair_sums(tasks, levels, lefts, lanes, values, col_n, col_s, row_n, row_s, half, unroll)
    for col in range(4):
        if col < first:
            out_n[col] = starts[0][col]
            out_s[col] = starts[1][col]
            continue
        n = fold_column(col_n, col - first, levels)
        s = fold_column(col_s, col - first, levels)
        if col < last:
            f = values[pl.ds((col - first) * (levels + 16) + 8, levels), :]
            itself = lax.rsqrt(jnp.maximum(0.0 * f, min_square)) - 1.0
            n = n + jnp.transpose(row_n[col - first])[:levels] - itself
            s = s + jnp.transpose(row_s[col - first])[:levels] - itself * f
        if first:
            n = n + starts[0][col]
            s = s + starts[1][col]
        out_n[col] = n
        out_s[col] = s


def far_kernel(raw, dom_raw, slab_raw, edge_raw, *refs, levels, half, unroll, slabs, doms):
    start_n, start_s, out_n, out_s, to_dom, to_slab, to_edge = refs[:7]
    parts, lanes, values, lefts, col_n, col_s, row_n, row_s = refs[7:]
    corner_x, corner_y = corners()
    next_slab = lax.axis_index("slab") + 1 < slabs
    next_dom = lax.axis_index("dom") + 1 < doms
    sources = (
        (dom_raw, 0, next_dom),
        (dom_raw, levels, next_dom),
        (slab_raw, 0, next_slab),
        (slab_raw, levels, next_slab),
        (edge_raw, 0, jnp.logical_and(next_slab, next_dom)),
    )
    for col, (source, base, valid) in enumerate(sources):
        make_lanes(source, base, col, levels, corner_x, corner_y, valid, parts, lanes, values)
    for row in range(3):
        make_rows(raw, (row + 1) * levels, row, levels, corner_x, corner_y, None, parts, lefts)
    make_rows(slab_raw, levels, 3, levels, corner_x, corner_y, next_slab, parts, lefts)
    pair_sums(
        far_tasks(), levels, lefts, lanes, values, col_n, col_s, row_n, row_s, half, unroll
    )
    for start, out, totals in ((start_n, out_n, row_n), (start_s, out_s, row_s)):
        out[0] = start[0]
        for row in range(3):
            out[row + 1] = start[row + 1] + jnp.transpose(totals[row])[:levels]
    for channel, (ref, totals) in enumerate(((col_n, row_n), (col_s, row_s))):
        for k in range(2):
            to_dom[channel, k] = jnp.where(next_dom, fold_column(ref, k, levels), 0.0)
        near = fold_column(ref, 2, levels)
        to_slab[channel, 0] = jnp.where(next_slab, near, 0.0)
        near = fold_column(ref, 3, levels) + jnp.transpose(totals[3])[:levels]
        to_slab[channel, 1] = jnp.where(next_slab, near, 0.0)
        near = fold_column(ref, 4, levels)
        to_edge[channel] = jnp.where(jnp.logical_and(next_slab, next_dom), near, 0.0)


def finish_kernel(raw, own_n, own_s, *refs, levels):
    from_dom, from_slab, from_edge, density, laplace = refs
    for col in range(4):
        sums = []
        for channel, near in enumerate((own_n, own_s)):
            total = near[col]
            if col in (0, 2):
                total = total + from_dom[channel, col // 2]
            if col in (0, 1):
                total = total + from_slab[channel, col]
            if col == 0:
                total = total + from_edge[channel]
            sums.append(total)
        filled = raw[pl.ds(col * levels * 4, levels, 4), :] > 0.5 * far_away
        n = jnp.where(filled, sums[0], 0.0)
        s = jnp.where(filled, sums[1], 0.0)
        f = raw[pl.ds(col * levels * 4 + 3, levels, 4), :]
        density[col] = n / ref_density
        laplace[col] = (s - f * n) / ref_density


def scratch_for(levels, cols, rows):
    span = levels + 2
    f32, bf16 = jnp.float32, jnp.bfloat16
    return [
        pltpu.VMEM((24, levels, 128), f32),
        pltpu.VMEM((4, cols * span, 16, 128), bf16),
        pltpu.VMEM((cols * (levels + 16), 128), f32),
        pltpu.VMEM((rows * levels, 32, 128), bf16),
        pltpu.VMEM((cols * span * 8, 128), f32),
        pltpu.VMEM((cols * span * 8, 128), f32),
        pltpu.VMEM((rows, 128, 128), f32),
        pltpu.VMEM((rows, 128, 128), f32),
    ]


def local(incoming, dest, counts):
    cells_x, cells_y, levels = counts.shape
    slots = incoming.shape[3]
    cells = cells_x * cells_y * levels
    capacity = cells // 4
    slabs, doms = lax.axis_size("slab"), lax.axis_size("dom")
    assert (cells_x, cells_y, slots) == (2, 2, 128) and levels % 8 == 0 and levels <= 128
    assert cells % 128 == 0 and cells <= 16 * 128 and doms >= 5
    assert capacity % 8 == 0 and 128 <= 4 * capacity <= 512
    f32, i32 = jnp.float32, jnp.int32
    shape = jax.ShapeDtypeStruct
    blocks = incoming.reshape(cells, 4, slots)
    *packs, stayed = pl.pallas_call(
        functools.partial(pack_kernel, cells=cells, capacity=capacity, domains=doms),
        out_shape=[shape((capacity + 1, 4, slots), f32)] * 4 + [shape((cells, 4, slots), f32)],
        in_specs=[vmem, vmem],
        out_specs=[vmem] * 5,
        scratch_shapes=[
            pltpu.VMEM((4 * capacity + cells, 4, slots), f32),
            pltpu.VMEM((cells // 128, 128), i32),
            pltpu.SMEM((cells // 128, 128), i32),
            pltpu.SemaphoreType.DMA,
        ],
        compiler_params=params,
        name="pack",
    )(dest.reshape(cells // 128, 128), blocks)
    got = [
        lax.ppermute(pack, "dom", [(i, (i + step) % doms) for i in range(doms)])
        for step, pack in zip(offsets, packs)
    ]
    column = (levels, 4, slots)
    home, to_dom, to_slab, to_edge = pl.pallas_call(
        functools.partial(place_kernel, cells=cells, capacity=capacity, levels=levels),
        out_shape=[shape((cells, 4, slots), f32)]
        + [shape((2 * levels, 4, slots), f32)] * 2
        + [shape(column, f32)],
        in_specs=[vmem] * 5 + [smem],
        out_specs=[vmem] * 4,
        scratch_shapes=[
            pltpu.VMEM((cells + 1, 4, slots), f32),
            pltpu.VMEM((4, 4, 128), i32),
            pltpu.SMEM((4, 4, 128), i32),
            pltpu.SemaphoreType.DMA,
        ],
        compiler_params=params,
        name="place",
    )(*got, stayed, counts)

    both = ("slab", "dom")

    def route(step_slab, step_dom):
        return [
            (s * doms + d, (s + step_slab) % slabs * doms + (d + step_dom) % doms)
            for s in range(slabs)
            for d in range(doms)
        ]

    def send(value, step_slab, step_dom):
        return lax.ppermute(value, both, route(step_slab, step_dom))

    def rows_of(value):
        return value.reshape(-1, slots)

    slab_raw = send(to_slab, -1, 0)
    dom_raw = send(to_dom, 0, -1)
    edge_raw = send(to_edge, -1, -1)
    raw = rows_of(home)
    half = 128
    plane = (4, levels, slots)

    def cost(tiles):
        return pl.CostEstimate(
            flops=levels * tiles * 128 * 128 * 600,
            bytes_accessed=cells * 4 * slots * 4,
            transcendentals=0,
        )

    def own_pairs(first, last, unroll, *start):
        return pl.pallas_call(
            functools.partial(
                own_kernel, levels=levels, half=half, unroll=unroll, first=first, last=last
            ),
            out_shape=[shape(plane, f32)] * 2,
            in_specs=[vmem] * (1 + len(start)),
            out_specs=[vmem] * 2,
            scratch_shapes=scratch_for(levels, 4 - first, last - first),
            compiler_params=params,
            cost_estimate=cost(26),
            name="own",
        )(raw, *start)

    early_n, early_s = own_pairs(0, 1, 8)
    far_n, far_s, ret_dom, ret_slab, ret_edge = pl.pallas_call(
        functools.partial(
            far_kernel, levels=levels, half=half, unroll=4, slabs=slabs, doms=doms
        ),
        out_shape=[shape(plane, f32)] * 2
        + [shape((2, 2, levels, slots), f32)] * 2
        + [shape((2, levels, slots), f32)],
        in_specs=[vmem] * 6,
        out_specs=[vmem] * 5,
        scratch_shapes=scratch_for(levels, 5, 4),
        compiler_params=params,
        cost_estimate=cost(30),
        name="far",
    )(raw, rows_of(dom_raw), rows_of(slab_raw), rows_of(edge_raw), early_n, early_s)
    from_slab = send(ret_slab, 1, 0)
    from_dom = send(ret_dom, 0, 1)
    from_edge = send(ret_edge, 1, 1)
    own_n, own_s = own_pairs(1, 4, 4, far_n, far_s)
    density, laplace = pl.pallas_call(
        functools.partial(finish_kernel, levels=levels),
        out_shape=[shape(plane, f32)] * 2,
        in_specs=[vmem] * 6,
        out_specs=[vmem] * 2,
        compiler_params=params,
        name="finish",
    )(raw, own_n, own_s, from_dom, from_slab, from_edge)
    final = (cells_x, cells_y, levels, slots)
    return density.reshape(final), laplace.reshape(final)


def solution(mesh):
    in_specs = (P("slab", "dom", None, None), P("slab", "dom"), P("slab", "dom", None))
    out_specs = (P("slab", "dom", None, None), P("slab", "dom", None, None))
    return jax.shard_map(local, mesh=mesh, in_specs=in_specs, out_specs=out_specs, check_vma=False)
```
